128 devices in a mesh: row: 16 (over z, y), col: 8 (over x, core).
Axes of the slice: x: 4, y: 4, z: 4, core: 2. Of those that a mesh axis runs over, the one named last changes fastest.
Arguments:
- hidden: bfloat16 [4096, 8192], P('row', 'col'), may hold values from -96 to 96
- norm_gain: bfloat16 [8192], P('col'), may hold values from 0.5 to 1.5
- w_query: bfloat16 [8192, 4096], P('row', 'col')
- w_key: bfloat16 [8192, 4096], P('row', 'col')
- w_value: bfloat16 [8192, 4096], P('row', 'col'), may hold values from -0.0625 to 0.0625
- w_out: bfloat16 [4096, 8192], P('row', 'col'), may hold values from -0.09375 to 0.09375
Outputs:
- context: bfloat16 [4096, 4096], P('row', 'col')
- layer_out: bfloat16 [4096, 8192], P('row', 'col')
The draws below stay inside these ranges and needn't reach their ends.
All inputs are finite; a program needn't handle non-finite values.
Results may differ from the reference program's by a relative error of at most 0.04.
Values may be sent and summed in bfloat16 or wider, within the bound.
A program may use at most 128 MiB of HBM per device.

```python
import math
import jax
import jax.numpy as jnp
from jax import lax

D = 8192
HEADS = 32
HD = 128
SEQ = 4096
N_ROW = 16


def draw_hidden(key, part):
    row_key = jax.random.fold_in(key, 21)
    column_key = jax.random.fold_in(key, 22)
    entry_key = jax.random.fold_in(key, 23)
    position = jnp.arange(D, dtype=jnp.float32) / max(D - 1, 1)
    entries = jnp.clip(jax.random.normal(entry_key, (SEQ, D), jnp.float32), -6.0, 6.0)
    trend = 0.5
    rough = jax.random.uniform(column_key, (D,), jnp.float32, 0.0, 0.5)
    column = 0.3 * jnp.exp(math.log(10.0) * (trend * position + rough))
    row_scale = 0.3 * jnp.exp(math.log(10.0) * jax.random.uniform(row_key, (SEQ, 1), jnp.float32, 0.0, 1.0))
    return (entries * column[None, :] * row_scale).astype(jnp.bfloat16)


def shared_keys(key):
    base = jax.random.normal(jax.random.fold_in(key, 7), (D, HEADS * HD), jnp.float32)
    return jnp.clip(base, -6.0, 6.0) * math.sqrt(2.0 / D)


def draw_w_key(key, part):
    return shared_keys(key).astype(jnp.bfloat16)


def draw_w_query(key, part):
    own = jnp.clip(jax.random.normal(jax.random.fold_in(key, 8), (D, HEADS * HD), jnp.float32), -6.0, 6.0) * math.sqrt(2.0 / D)
    return own.astype(jnp.bfloat16)


def levels(stream_key, dims, shards, low, top_value):
    def one(dim, parts):
        draws = jax.random.uniform(jax.random.fold_in(jax.random.fold_in(stream_key, 6), dim), (parts,), jnp.float32, low / len(shards), top_value / len(shards))
        return jnp.repeat(jnp.exp(draws), dims[dim] // parts).reshape((-1,) + (1,) * (len(dims) - dim - 1))

    level = one(*shards[0])
    for cut in shards[1:]:
        level = level * one(*cut)
    return level


def gaussian(rng, dims, scale, most, cuts=(), kind=jnp.bfloat16):
    drawn = jax.random.normal(rng, dims, jnp.float32) * scale
    if len(cuts) > 0:
        drawn = levels(rng, dims, cuts, -0.22, 0.18) * drawn
    return jnp.clip(drawn, min=-most, max=most).astype(kind)


def setup_inputs(seed: int = 0) -> dict:
    arg_keys = jax.random.split(jax.random.key(seed), 7)
    return {
        "hidden": draw_hidden(jax.random.fold_in(arg_keys[6], 71), 0),
        "norm_gain": jnp.clip(1.0 + 0.1 * jax.random.normal(arg_keys[1], (D,), jnp.float32), 0.5, 1.5).astype(jnp.bfloat16),
        "w_query": draw_w_query(jax.random.fold_in(arg_keys[6], 71), 0),
        "w_key": draw_w_key(jax.random.fold_in(arg_keys[6], 71), 0),
        "w_value": gaussian(arg_keys[4], (D, HEADS * HD), D ** -0.5, 0.0625, ((0, 16), (1, 8))),
        "w_out": gaussian(arg_keys[5], (HEADS * HD, D), (HEADS * HD) ** -0.5, 0.09375, ((0, 16), (1, 8))),
    }


def rotary(values, positions):
    half = values.shape[-1] // 2
    freqs = jnp.exp(-math.log(10000.0) * 2.0 * jnp.arange(half, dtype=jnp.float32) / values.shape[-1])
    angles = positions.astype(jnp.float32)[:, None] * freqs[None, :]
    cosine = jnp.cos(angles)[:, None, :]
    sine = jnp.sin(angles)[:, None, :]
    first = values[..., :half]
    second = values[..., half:]
    return jnp.concatenate((first * cosine - second * sine, second * cosine + first * sine), axis=-1)

def blockwise(left, right):
    width = left.shape[1] // N_ROW
    total = jnp.zeros((left.shape[0], right.shape[1]), jnp.float32)
    for index in range(N_ROW):
        part = jnp.dot(left[:, index * width:(index + 1) * width], right[index * width:(index + 1) * width], preferred_element_type=jnp.float32)
        total = total + lax.optimization_barrier(part.astype(jnp.bfloat16)).astype(jnp.float32)
    return total

def one_head(operands):
    query, key, value = operands
    scores = jnp.dot(query, key.T, preferred_element_type=jnp.float32) * (1.0 / math.sqrt(HD))
    length = query.shape[0]
    allowed = jnp.arange(length, dtype=jnp.int32)[None, :] <= jnp.arange(length, dtype=jnp.int32)[:, None]
    scores = jnp.where(allowed, scores, -jnp.inf)
    peak = lax.optimization_barrier(jnp.max(scores, axis=1, keepdims=True))
    probs = jnp.exp(scores - peak)
    totals = lax.optimization_barrier(jnp.sum(probs, axis=1, keepdims=True))
    weighted = jnp.dot(probs.astype(jnp.bfloat16), value, preferred_element_type=jnp.float32)
    return (weighted / totals).astype(jnp.bfloat16)

def reference(hidden, norm_gain, w_query, w_key, w_value, w_out):
    residual = hidden.astype(jnp.float32)
    mean_square = lax.optimization_barrier(jnp.mean(residual * residual, axis=1, keepdims=True))
    normed = (residual * lax.rsqrt(mean_square + 1e-05) * norm_gain.astype(jnp.float32)[None, :]).astype(jnp.bfloat16)
    proj_q = blockwise(normed, w_query)
    proj_k = blockwise(normed, w_key)
    proj_v = blockwise(normed, w_value)
    length = hidden.shape[0]
    heads = w_query.shape[1] // HD
    positions = jnp.arange(length, dtype=jnp.int32)
    query = rotary(proj_q.reshape(length, heads, HD), positions).astype(jnp.bfloat16)
    key = rotary(proj_k.reshape(length, heads, HD), positions).astype(jnp.bfloat16)
    value = proj_v.astype(jnp.bfloat16).reshape(length, heads, HD)
    per_head = lax.map(one_head, (query.transpose(1, 0, 2), key.transpose(1, 0, 2), value.transpose(1, 0, 2)))
    context = per_head.transpose(1, 0, 2).reshape(length, heads * HD)
    attended = blockwise(context, w_out)
    layer_out = (residual + attended).astype(jnp.bfloat16)
    return (context, layer_out)
```

```python
import math

import jax
import jax.numpy as jnp
import numpy as np
from jax import lax
from jax.experimental import pallas as pl
from jax.experimental.pallas import tpu as pltpu
from jax.sharding import Mesh, PartitionSpec as P

HD = 128
EPS = 1e-5
MESH = pl.DeviceIdType.MESH
BF = jnp.bfloat16
F32 = jnp.float32


def rotary_tables(block, blocks):
    freqs = np.exp(-math.log(10000.0) * 2.0 * np.arange(HD // 2) / HD)
    freqs = np.concatenate([freqs, freqs])[None, :]
    base = (np.arange(blocks) * block)[:, None] * freqs
    rows = np.arange(block)[:, None] * freqs
    angles = np.concatenate([base, rows], axis=0)
    return np.concatenate([np.cos(angles), np.sin(angles)], axis=1).astype(np.float32)


class Ids:
    def __init__(self):
        self.table = {}

    def __call__(self, *name):
        return self.table.setdefault(name, len(self.table))


N_MESSAGES = 160


def kernel(
    features, hidden, gain, wq, wk, wv, wout, tables,
    ctx_out, layer_out,
    xg, gbuf, xs, ssq, sqs, rsc, wg, pbuf, tr, fin, kvg, qbuf, sbuf,
    cown, ctxs, cx, wog, op, otr, ofin, send_sem, recv_sem, local_sem,
):
    z, y, x, c = (lax.axis_index(n) for n in ("z", "y", "x", "c"))
    zr, zl, zf = (lax.rem(z + k, 4) for k in (1, 3, 2))
    yr, yl, yf = (lax.rem(y + k, 4) for k in (1, 3, 2))
    xr, xl, xf = (lax.rem(x + k, 4) for k in (1, 3, 2))
    other = 1 - c
    block = hidden.shape[0]
    half = block // 2
    ids = Ids()
    sends = []

    def message(src, dst, name, **where):
        i = ids(*name)
        return pltpu.make_async_remote_copy(
            src_ref=src, dst_ref=dst, send_sem=send_sem.at[i], recv_sem=recv_sem.at[i],
            device_id=where, device_id_type=MESH,
        )

    def send(src, dst, name, **where):
        copy = message(src, dst, name, **where)
        copy.start()
        sends.append(copy)

    def arrived(dst, name, **where):
        message(dst, dst, name, **where).wait_recv()

    barrier = pltpu.get_barrier_semaphore()
    partners = [{"z": zr}, {"z": zl}, {"z": zf}, {"y": yr}, {"y": yl}, {"x": xr}, {"x": xl}, {"c": other}]
    for where in partners:
        pl.semaphore_signal(barrier, inc=1, device_id=where, device_id_type=MESH)

    @pl.when(x != z)
    def _():
        pl.semaphore_signal(barrier, inc=1, device_id={"z": x, "x": z}, device_id_type=MESH)

    pl.semaphore_wait(barrier, len(partners) + jnp.where(x != z, 1, 0))

    def swap_start(src, dst, name):
        copy = message(src, dst, name, z=x, x=z)
        local = pltpu.make_async_copy(src, dst, local_sem.at[ids(*name)])

        @pl.when(x != z)
        def _():
            copy.start()

        @pl.when(x == z)
        def _():
            local.start()

    def swap_arrived(src, dst, name):
        copy = message(src, dst, name, z=x, x=z)
        local = pltpu.make_async_copy(src, dst, local_sem.at[ids(*name)])

        @pl.when(x != z)
        def _():
            copy.wait_recv()
            copy.wait_send()

        @pl.when(x == z)
        def _():
            local.wait()

    def gather_y(slot, name):
        send(slot(y, None), slot(y, None), (name, "r"), y=yr)
        send(slot(y, None), slot(y, None), (name, "l"), y=yl)

    def forward_y(slot, name):
        arrived(slot(yl, None), (name, "r"), y=yr)
        send(slot(yl, 0), slot(yl, 0), (name, "fr"), y=yr)
        arrived(slot(yr, None), (name, "l"), y=yl)
        send(slot(yr, 1), slot(yr, 1), (name, "fl"), y=yl)

    def finish_y(slot, name):
        arrived(slot(yf, 0), (name, "fr"), y=yr)
        arrived(slot(yf, 1), (name, "fl"), y=yl)

    weights = {"k": wk, "v": wv, "q": wq}
    order = {"k": 0, "v": 1, "q": 2}
    wrows = wk.shape[0]

    def weight_slot(name):
        def slot(owner, part):
            ref = wg.at[order[name], owner]
            return ref if part is None else ref.at[pl.ds(part * (wrows // 2), wrows // 2)]
        return slot

    def weight_gather(name):
        mine = weights[name]
        dst = weight_slot(name)(y, None)
        send(mine, dst, ("w" + name, "r"), y=yr)
        send(mine, dst, ("w" + name, "l"), y=yl)

    def rows(ref, h):
        return ref.at[pl.ds(h * half, half)]

    def x_slot(plane, t, h):
        return rows(xg.at[plane, t], h)

    weight_gather("k")
    for h in range(2):
        swap_start(rows(hidden, h), x_slot(c, z, h), ("xp", h))
    swap_start(gain, gbuf.at[c], ("gp",))
    weight_gather("v")
    local_w = []
    for name in "kvq":
        copy = pltpu.make_async_copy(weights[name], wg.at[order[name], y], local_sem.at[ids("lw", name)])
        copy.start()
        local_w.append(copy)

    def process(plane, t, first):
        g = gbuf[plane].astype(F32)
        width = g.shape[1]

        @pl.loop(0, block // 32)
        def _(i):
            r = pl.ds(pl.multiple_of(i * 32, 32), 32)
            v = xg[plane, t, r, :].astype(F32)
            xs[plane, t, r, :] = (v * g).astype(BF)
            sq = v * v
            total = sq[:, :HD]
            for k in range(1, width // HD):
                total = total + sq[:, k * HD:(k + 1) * HD]
            if first:
                ssq[t, r, :] = total
            else:
                ssq[t, r, :] = ssq[t, r, :] + total

    def pair_send(t, label, h):
        send(x_slot(c, t, h), x_slot(c, t, h), ("pair", label, h), c=other)

    swap_arrived(gain, gbuf.at[c], ("gp",))
    send(gbuf.at[c], gbuf.at[c], ("gpair",), c=other)
    for h in range(2):
        swap_arrived(rows(hidden, h), x_slot(c, x, h), ("xp", h))
        send(x_slot(c, x, h), x_slot(c, x, h), ("xr", h), x=xr)
        send(x_slot(c, x, h), x_slot(c, x, h), ("xl", h), x=xl)
        pair_send(x, "own", h)
    forward_y(weight_slot("k"), "wk")
    process(c, x, True)
    arrived(x_slot(c, xl, 0), ("xr", 0), x=xr)
    send(x_slot(c, xl, 0), x_slot(c, xl, 0), ("xfr",), x=xr)
    pair_send(xl, "left", 0)
    arrived(x_slot(c, xr, 0), ("xl", 0), x=xl)
    pair_send(xr, "right", 0)
    forward_y(weight_slot("v"), "wv")
    weight_gather("q")
    arrived(x_slot(c, xr, 1), ("xl", 1), x=xl)
    send(x_slot(c, xr, 1), x_slot(c, xr, 1), ("xfl",), x=xl)
    pair_send(xr, "right", 1)
    arrived(x_slot(c, xl, 1), ("xr", 1), x=xr)
    pair_send(xl, "left", 1)
    arrived(gbuf.at[other], ("gpair",), c=other)
    process(c, xr, True)
    process(c, xl, True)
    for h in range(2):
        arrived(x_slot(other, x, h), ("pair", "own", h), c=other)
    process(other, x, False)
    arrived(x_slot(c, xf, 0), ("xfr",), x=xr)
    pair_send(xf, "far", 0)
    arrived(x_slot(c, xf, 1), ("xfl",), x=xl)
    pair_send(xf, "far", 1)
    process(c, xf, True)
    for t, label in ((xr, "right"), (xl, "left"), (xf, "far")):
        for h in range(2):
            arrived(x_slot(other, t, h), ("pair", label, h), c=other)
        process(other, t, False)
    for t in range(4):
        s = jnp.sum(ssq[t].T, axis=0, keepdims=True)
        sqs[z, t] = jnp.broadcast_to(s, (8, block))
    for where, label in ((zr, 1), (zl, 3), (zf, 2)):
        send(sqs.at[z], sqs.at[z], ("sq", label), z=where)

    cw = wk.shape[1]

    def lower(ref):
        return ref.at[pl.ds(0, 2 * block)]

    def upper(ref):
        return ref.at[pl.ds(2 * block, 2 * block)]

    def project(name):
        j = order[name]
        width = xs.shape[3]
        tokens = 4 * block

        @pl.loop(0, cw // 256)
        def _(n):
            cols = pl.ds(pl.multiple_of(n * 256, 256), 256)
            w0 = wg[j, 0:2, :, cols].reshape(width, 256)
            w1 = wg[j, 2:4, :, cols].reshape(width, 256)
            left0 = xs[0].reshape(tokens, width)
            left1 = xs[1].reshape(tokens, width)
            acc = jnp.dot(left0, w0, preferred_element_type=F32)
            acc = acc + jnp.dot(left1, w1, preferred_element_type=F32)
            pbuf[j, 2 * n] = acc[:, :HD].astype(BF)
            pbuf[j, 2 * n + 1] = acc[:, HD:].astype(BF)

        send(lower(pbuf.at[j, zf]), tr.at[j, 0], (name, "ta"), z=zr)
        send(upper(pbuf.at[j, zf]), tr.at[j, 1], (name, "tb"), z=zl)
        send(upper(pbuf.at[j, zr]), upper(fin.at[j, 0]), (name, "a1"), z=zr)
        send(lower(pbuf.at[j, zl]), lower(fin.at[j, 1]), (name, "b0"), z=zl)

    def relay(name):
        j = order[name]
        lo, hi = pl.ds(0, 2 * block), pl.ds(2 * block, 2 * block)
        arrived(tr.at[j, 0], (name, "ta"), z=zr)
        pbuf[j, zr, lo, :] = (pbuf[j, zr, lo, :].astype(F32) + tr[j, 0].astype(F32)).astype(BF)
        send(lower(pbuf.at[j, zr]), lower(fin.at[j, 0]), (name, "a0"), z=zr)
        arrived(tr.at[j, 1], (name, "tb"), z=zl)
        pbuf[j, zl, hi, :] = (pbuf[j, zl, hi, :].astype(F32) + tr[j, 1].astype(F32)).astype(BF)
        send(upper(pbuf.at[j, zl]), upper(fin.at[j, 1]), (name, "b1"), z=zl)

    def reduced(name):
        j = order[name]
        arrived(upper(fin.at[j, 0]), (name, "a1"), z=zr)
        arrived(lower(fin.at[j, 1]), (name, "b0"), z=zl)
        arrived(lower(fin.at[j, 0]), (name, "a0"), z=zr)
        arrived(upper(fin.at[j, 1]), (name, "b1"), z=zl)

    def total_of(name, t):
        j = order[name]
        r = pl.ds(t * block, block)
        total = pbuf[j, z, r, :].astype(F32) + fin[j, 0, r, :].astype(F32) + fin[j, 1, r, :].astype(F32)
        return total * rsc[r, :]

    def rotated(v, t):
        bases = tables[:16, :]
        here = lax.broadcasted_iota(jnp.int32, bases.shape, 0) == 4 * t + y
        base = jnp.sum(jnp.where(here, bases, 0.0), axis=0, keepdims=True)
        ca, sa = base[:, :HD], base[:, HD:]
        ci, si = tables[16:, :HD], tables[16:, HD:]
        cos = ca * ci - sa * si
        sin = sa * ci + ca * si
        lane = lax.broadcasted_iota(jnp.int32, (block, HD), 1)
        signed = jnp.where(lane < HD // 2, -sin, sin)
        return v * cos + pltpu.roll(v, HD // 2, axis=1) * signed

    for copy in local_w:
        copy.wait()
    finish_y(weight_slot("k"), "wk")
    project("k")
    finish_y(weight_slot("v"), "wv")
    project("v")
    forward_y(weight_slot("q"), "wq")
    relay("k")

    for where, label in ((zr, 1), (zl, 3), (zf, 2)):
        src = {1: zl, 3: zr, 2: zf}[label]
        arrived(sqs.at[src], ("sq", label), z=where)
    for t in range(4):
        s = sqs[0, t] + sqs[1, t] + sqs[2, t] + sqs[3, t]
        factor = lax.rsqrt(s / features + EPS)
        rsc[pl.ds(t * block, block), :] = jnp.broadcast_to(factor[0:1, :], (HD, block)).T

    def kv_slot(which):
        def slot(owner, part):
            ref = kvg.at[which]
            return ref.at[:, owner] if part is None else ref.at[pl.ds(2 * part, 2), owner]
        return slot

    def out_slot(owner, part):
        ref = wog.at[owner]
        count = wout.shape[0] // 2
        return ref if part is None else ref.at[pl.ds(part * count, count)]

    relay("v")
    reduced("k")
    for t in range(4):
        kvg[0, t, y] = rotated(total_of("k", t), t).astype(BF)
    gather_y(kv_slot(0), "k")
    finish_y(weight_slot("q"), "wq")
    project("q")
    reduced("v")
    for t in range(4):
        kvg[1, t, y] = total_of("v", t).astype(BF)
    gather_y(kv_slot(1), "v")
    relay("q")
    forward_y(kv_slot(0), "k")
    forward_y(kv_slot(1), "v")
    send(wout, wog.at[y], ("wo", "r"), y=yr)
    send(wout, wog.at[y], ("wo", "l"), y=yl)
    wo_copy = pltpu.make_async_copy(wout, wog.at[y], local_sem.at[ids("lwo")])
    wo_copy.start()
    reduced("q")
    for t in range(4):
        qbuf[t] = rotated(total_of("q", t), t).astype(BF)
    finish_y(kv_slot(0), "k")
    finish_y(kv_slot(1), "v")

    factor = math.log2(math.e) / math.sqrt(HD)
    span = 4 * block

    def keys(which, kb):
        return kvg[which, kb].reshape(span, HD)

    def cx_slot(plane, owner, t):
        return cx.at[plane, owner, pl.ds(t * block, block)]

    heads_base = [ids("c2", k) for k in range(4)][0]

    def head_copy(src, dst, target, source):
        return pltpu.make_async_remote_copy(
            src_ref=src, dst_ref=dst, send_sem=send_sem.at[heads_base + target],
            recv_sem=recv_sem.at[heads_base + source], device_id={"z": target}, device_id_type=MESH,
        )

    def context_sends(t):
        mine = cown.at[pl.ds(t * block, block)]

        @pl.when(z != t)
        def _():
            head_copy(mine, ctxs.at[z], t, z).start()

        @pl.when(z == t)
        def _():
            ctxs[z] = cown[pl.ds(t * block, block), :]

        swap_start(mine, cx_slot(c, z, t), ("cp", t))

    for t in range(4):
        q = qbuf[t]

        def score(kb, peak):
            s = lax.dot_general(q, keys(0, kb), (((1,), (1,)), ((), ())), preferred_element_type=F32)
            sbuf[kb] = s
            return jnp.maximum(peak, jnp.max(s, axis=1, keepdims=True))

        peak = jnp.full((block, 1), -1e30, F32)
        if t > 0:
            peak = lax.fori_loop(0, t, score, peak)
        s = lax.dot_general(q, keys(0, t), (((1,), (1,)), ((), ())), preferred_element_type=F32)
        row = lax.broadcasted_iota(jnp.int32, (block, span), 0) + y * block
        col = lax.broadcasted_iota(jnp.int32, (block, span), 1)
        s = jnp.where(col <= row, s, -jnp.inf)
        sbuf[t] = s
        peak = jnp.maximum(peak, jnp.max(s, axis=1, keepdims=True))

        def weigh(kb, carry):
            total, acc = carry
            p = jnp.exp2((sbuf[kb] - peak) * factor)
            total = total + jnp.sum(p, axis=1, keepdims=True)
            acc = acc + jnp.dot(p.astype(BF), keys(1, kb), preferred_element_type=F32)
            return total, acc

        total, acc = lax.fori_loop(
            0, t + 1, weigh, (jnp.zeros((block, 1), F32), jnp.zeros((block, HD), F32))
        )
        cown[pl.ds(t * block, block), :] = (acc / total).astype(BF)
        context_sends(t)
        if t == 1:
            forward_y(out_slot, "wo")

    def cx_part(plane, owner, h):
        return cx.at[plane, owner, pl.ds(2 * h * block, 2 * block)]

    for h in range(2):
        for t in (2 * h, 2 * h + 1):
            mine = cown.at[pl.ds(t * block, block)]
            swap_arrived(mine, cx_slot(c, x, t), ("cp", t))
        send(cx_part(c, x, h), cx_part(c, x, h), ("cr", h), x=xr)
        send(cx_part(c, x, h), cx_part(c, x, h), ("cl", h), x=xl)
        send(cx_part(c, x, h), cx_part(c, x, h), ("cpair", "own", h), c=other)

    def cx_pair(owner, label, h):
        send(cx_part(c, owner, h), cx_part(c, owner, h), ("cpair", label, h), c=other)

    arrived(cx_part(c, xl, 0), ("cr", 0), x=xr)
    send(cx_part(c, xl, 0), cx_part(c, xl, 0), ("cfr",), x=xr)
    cx_pair(xl, "left", 0)
    arrived(cx_part(c, xr, 0), ("cl", 0), x=xl)
    cx_pair(xr, "right", 0)
    arrived(cx_part(c, xr, 1), ("cl", 1), x=xl)
    send(cx_part(c, xr, 1), cx_part(c, xr, 1), ("cfl",), x=xl)
    cx_pair(xr, "right", 1)
    arrived(cx_part(c, xl, 1), ("cr", 1), x=xr)
    cx_pair(xl, "left", 1)

    for h in range(4):
        @pl.when(z != h)
        def _():
            copy = head_copy(cown.at[pl.ds(h * block, block)], ctxs.at[h], h, h)
            copy.wait_send()
            copy.wait_recv()

    for h in range(4):
        ctx_out[:, h * HD:(h + 1) * HD] = ctxs[h]

    wo_copy.wait()
    finish_y(out_slot, "wo")
    arrived(cx_part(c, xf, 0), ("cfr",), x=xr)
    cx_pair(xf, "far", 0)
    arrived(cx_part(c, xf, 1), ("cfl",), x=xl)
    cx_pair(xf, "far", 1)
    for label, owner in (("own", x), ("left", xl), ("right", xr), ("far", xf)):
        for h in range(2):
            arrived(cx_part(other, owner, h), ("cpair", label, h), c=other)

    def out_product(d):
        r = pl.ds(pl.multiple_of(d * block, block), block)
        left = jnp.concatenate([cx[p, k, r, :] for p in range(2) for k in range(4)], axis=1)
        right = wog[...].reshape(left.shape[1], wog.shape[2])
        return jnp.dot(left, right, preferred_element_type=F32)

    def first(ref):
        return ref.at[pl.ds(0, half)]

    def second(ref):
        return ref.at[pl.ds(half, half)]

    op[zf] = out_product(zf).astype(BF)
    send(first(op.at[zf]), otr.at[0], ("o", "ta"), z=zr)
    send(second(op.at[zf]), otr.at[1], ("o", "tb"), z=zl)
    op[zr] = out_product(zr).astype(BF)
    send(second(op.at[zr]), second(ofin.at[0]), ("o", "a1"), z=zr)
    op[zl] = out_product(zl).astype(BF)
    send(first(op.at[zl]), first(ofin.at[1]), ("o", "b0"), z=zl)
    lo, hi = pl.ds(0, half), pl.ds(half, half)
    arrived(otr.at[0], ("o", "ta"), z=zr)
    op[zr, lo, :] = (op[zr, lo, :].astype(F32) + otr[0].astype(F32)).astype(BF)
    send(first(op.at[zr]), first(ofin.at[0]), ("o", "a0"), z=zr)
    arrived(otr.at[1], ("o", "tb"), z=zl)
    op[zl, hi, :] = (op[zl, hi, :].astype(F32) + otr[1].astype(F32)).astype(BF)
    send(second(op.at[zl]), second(ofin.at[1]), ("o", "b1"), z=zl)
    oacc = hidden[...].astype(F32) + out_product(z)
    arrived(second(ofin.at[0]), ("o", "a1"), z=zr)
    arrived(first(ofin.at[1]), ("o", "b0"), z=zl)
    arrived(first(ofin.at[0]), ("o", "a0"), z=zr)
    arrived(second(ofin.at[1]), ("o", "b1"), z=zl)
    layer_out[...] = (oacc + ofin[0].astype(F32) + ofin[1].astype(F32)).astype(BF)
    for copy in sends:
        copy.wait_send()


def on_device(hidden, norm_gain, w_query, w_key, w_value, w_out):
    block, width = hidden.shape
    wrows, cw = w_query.shape
    orows, ow = w_out.shape
    features = 8 * width
    tables = jnp.asarray(rotary_tables(block, 16))
    vmem = pl.BlockSpec(memory_space=pltpu.VMEM)

    def body(*refs):
        kernel(features, *refs)

    return pl.pallas_call(
        body,
        out_shape=(
            jax.ShapeDtypeStruct((block, cw), BF),
            jax.ShapeDtypeStruct((block, ow), BF),
        ),
        in_specs=[vmem] * 7,
        out_specs=(vmem, vmem),
        scratch_shapes=[
            pltpu.VMEM((2, 4, block, width), BF),
            pltpu.VMEM((2, 1, width), BF),
            pltpu.VMEM((2, 4, block, width), BF),
            pltpu.VMEM((4, block, HD), F32),
            pltpu.VMEM((4, 4, 8, block), F32),
            pltpu.VMEM((4 * block, HD), F32),
            pltpu.VMEM((3, 4, wrows, cw), BF),
            pltpu.VMEM((3, 4, 4 * block, HD), BF),
            pltpu.VMEM((3, 2, 2 * block, HD), BF),
            pltpu.VMEM((3, 2, 4 * block, HD), BF),
            pltpu.VMEM((2, 4, 4, block, HD), BF),
            pltpu.VMEM((4, block, HD), BF),
            pltpu.VMEM((4, block, 4 * block), F32),
            pltpu.VMEM((4 * block, HD), BF),
            pltpu.VMEM((4, block, HD), BF),
            pltpu.VMEM((2, 4, 4 * block, HD), BF),
            pltpu.VMEM((4, orows, ow), BF),
            pltpu.VMEM((4, block, ow), BF),
            pltpu.VMEM((2, block // 2, ow), BF),
            pltpu.VMEM((2, block, ow), BF),
            pltpu.SemaphoreType.DMA((N_MESSAGES,)),
            pltpu.SemaphoreType.DMA((N_MESSAGES,)),
            pltpu.SemaphoreType.DMA((N_MESSAGES,)),
        ],
        compiler_params=pltpu.CompilerParams(
            collective_id=0, has_side_effects=True, vmem_limit_bytes=62 * 1024 * 1024
        ),
    )(hidden, norm_gain.reshape(1, width), w_query, w_key, w_value, w_out, tables)


def solution(mesh):
    cube = Mesh(mesh.devices.reshape(4, 4, 4, 2), ("z", "y", "x", "c"))
    rows, cols = ("z", "y"), ("x", "c")
    both = P(rows, cols)
    return jax.shard_map(
        on_device,
        mesh=cube,
        in_specs=(both, P(cols), both, both, both, both),
        out_specs=(both, both),
        check_vma=False,
    )
```

```python
import math

import jax
import jax.numpy as jnp
import numpy as np
from jax import lax
from jax.experimental import pallas as pl
from jax.experimental.pallas import tpu as pltpu
from jax.sharding import Mesh, PartitionSpec as P

HD = 128
EPS = 1e-5
MESH = pl.DeviceIdType.MESH
BF = jnp.bfloat16
F32 = jnp.float32


def rotary_tables(block, blocks):
    freqs = np.exp(-math.log(10000.0) * 2.0 * np.arange(HD // 2) / HD)
    freqs = np.concatenate([freqs, freqs])[None, :]
    base = (np.arange(blocks) * block)[:, None] * freqs
    rows = np.arange(block)[:, None] * freqs
    angles = np.concatenate([base, rows], axis=0)
    return np.concatenate([np.cos(angles), np.sin(angles)], axis=1).astype(np.float32)


class Ids:
    def __init__(self):
        self.table = {}

    def __call__(self, *name):
        return self.table.setdefault(name, len(self.table))


N_MESSAGES = 160


def kernel(
    features, hidden, wq, wk, wv, wout, gain, tables,
    ctx_out, layer_out,
    big, transit, gbuf, xs, ssq, sqs, rsc, wg, pbuf, tr, fin, kvg, qbuf, sbuf,
    cbig, ctransit, ctxs, wog, op, otr, ofin, send_sem, recv_sem, local_sem,
):
    z, y, x, c = (lax.axis_index(n) for n in ("z", "y", "x", "c"))
    zr, zl, zf = (lax.rem(z + k, 4) for k in (1, 3, 2))
    yr, yl, yf = (lax.rem(y + k, 4) for k in (1, 3, 2))
    xr, xl, xf = (lax.rem(x + k, 4) for k in (1, 3, 2))
    other = 1 - c
    block = hidden.shape[0]
    half = block // 2
    ids = Ids()
    sends = []

    def message(src, dst, name, **where):
        i = ids(*name)
        return pltpu.make_async_remote_copy(
            src_ref=src, dst_ref=dst, send_sem=send_sem.at[i], recv_sem=recv_sem.at[i],
            device_id=where, device_id_type=MESH,
        )

    def send(src, dst, name, **where):
        copy = message(src, dst, name, **where)
        copy.start()
        sends.append(copy)

    def arrived(dst, name, **where):
        message(dst, dst, name, **where).wait_recv()

    barrier = pltpu.get_barrier_semaphore()
    partners = [{"z": zr}, {"z": zl}, {"z": zf}, {"y": yr}, {"y": yl}, {"x": xr}, {"x": xl}, {"c": other}]
    for where in partners:
        pl.semaphore_signal(barrier, inc=1, device_id=where, device_id_type=MESH)

    def load(src, dst, name):
        copy = pltpu.make_async_copy(src, dst, local_sem.at[ids("load", name)])
        copy.start()
        return copy

    weights = {"k": wk, "v": wv, "q": wq}
    order = {"k": 0, "v": 1, "q": 2}
    loads = {"x": load(hidden, big.at[x], "x")}
    for name in "kvq":
        loads[name] = load(weights[name], wg.at[order[name], y], name)
    loads["o"] = load(wout, wog.at[y], "o")
    pl.semaphore_wait(barrier, len(partners))

    def gather_y(slot, name):
        send(slot(y, None), slot(y, None), (name, "r"), y=yr)
        send(slot(y, None), slot(y, None), (name, "l"), y=yl)

    def forward_y(slot, name):
        arrived(slot(yl, None), (name, "r"), y=yr)
        send(slot(yl, 0), slot(yl, 0), (name, "fr"), y=yr)
        arrived(slot(yr, None), (name, "l"), y=yl)
        send(slot(yr, 1), slot(yr, 1), (name, "fl"), y=yl)

    def finish_y(slot, name):
        arrived(slot(yf, 0), (name, "fr"), y=yr)
        arrived(slot(yf, 1), (name, "fl"), y=yl)

    wrows = wk.shape[0]

    def weight_slot(name):
        def slot(owner, part):
            ref = wg.at[order[name], owner]
            return ref if part is None else ref.at[pl.ds(part * (wrows // 2), wrows // 2)]
        return slot

    class Spread:
        def __init__(self, name, buf, through):
            self.name, self.buf, self.through = name, buf, through
            self.rows = buf.shape[1] // 2

        def part(self, slot, h):
            return self.buf.at[slot, pl.ds(h * self.rows, self.rows)]

        def own(self, h):
            mine = self.part(x, h)
            send(mine, mine, (self.name, "xr", h), x=xr)
            send(mine, mine, (self.name, "xl", h), x=xl)
            self.onward(0, h)

        def pair(self, src_slot, owner, label, h):
            send(self.part(src_slot, h), self.part(8 + owner, h), (self.name, "pair", label, h), c=other)

        def onward(self, k, h):
            owner = lax.rem(x + k, 4)
            away = lax.rem(owner - z + 4, 4)
            src = self.part(owner, h)

            @pl.when(away == 0)
            def _():
                message(src, self.part(8 + z, h), (self.name, "pair", "own", h), c=other).start()

            @pl.when(away == 1)
            def _():
                message(src, self.part(4 + z, h), (self.name, "zr", h), z=zr).start()

            @pl.when(away == 3)
            def _():
                message(src, self.part(4 + z, h), (self.name, "zl", h), z=zl).start()

            @pl.when(away == 2)
            def _():
                to = {"z": zl} if h else {"z": zr}
                message(src, self.through.at[h], (self.name, "zz", h), **to).start()

            if k == 0:
                for label, where in (("zr", {"z": zr}), ("zl", {"z": zl}), ("zz", {"z": zl} if h else {"z": zr})):
                    sends.append(message(self.part(0, h), self.part(0, h), (self.name, label, h), **where))
                sends.append(message(self.part(0, h), self.part(0, h), (self.name, "pair", "own", h), c=other))

        def from_left(self, h):
            mine = self.part(xl, h)
            arrived(mine, (self.name, "xr", h), x=xr)
            if h == 0:
                send(mine, mine, (self.name, "xf", 0), x=xr)
            self.onward(3, h)

        def from_right(self, h):
            mine = self.part(xr, h)
            arrived(mine, (self.name, "xl", h), x=xl)
            if h == 1:
                send(mine, mine, (self.name, "xf", 1), x=xl)
            self.onward(1, h)

        def from_far(self, h):
            where = {"x": xl} if h else {"x": xr}
            arrived(self.part(xf, h), (self.name, "xf", h), **where)
            self.onward(2, h)

        def pass_on(self, h):
            where = {"z": zl} if h else {"z": zr}
            arrived(self.through.at[h], (self.name, "zz", h), **where)
            send(self.through.at[h], self.part(4 + (zr if h else zl), h), (self.name, "zf", h), **where)

        def beside(self, which, h):
            owner, where = (zl, {"z": zr}) if which == "zr" else (zr, {"z": zl})
            arrived(self.part(4 + owner, h), (self.name, which, h), **where)
            self.pair(4 + owner, owner, which, h)

        def opposite(self, h):
            where = {"z": zl} if h else {"z": zr}
            arrived(self.part(4 + zf, h), (self.name, "zf", h), **where)
            self.pair(4 + zf, zf, "zf", h)

        def paired(self, owner, label):
            for h in range(2):
                arrived(self.part(8 + owner, h), (self.name, "pair", label, h), c=other)

    def process(slot, plane, t, first):
        g = gbuf[z, plane].astype(F32)
        width = g.shape[1]

        @pl.loop(0, block // 32)
        def _(i):
            r = pl.ds(pl.multiple_of(i * 32, 32), 32)
            v = big[slot, r, :].astype(F32)
            xs[plane, t, r, :] = (v * g).astype(BF)
            sq = v * v
            total = sq[:, :HD]
            for k in range(1, width // HD):
                total = total + sq[:, k * HD:(k + 1) * HD]
            if first:
                ssq[t, r, :] = total
            else:
                ssq[t, r, :] = ssq[t, r, :] + total

    spread = Spread("h", big, transit)
    loads["x"].wait()
    for h in range(2):
        spread.own(h)
    loads["k"].wait()
    gather_y(weight_slot("k"), "wk")
    loads["v"].wait()
    gather_y(weight_slot("v"), "wv")
    gain_copy = pltpu.make_async_copy(gain, gbuf.at[x, c], local_sem.at[ids("gain")])
    gain_copy.start()
    gain_sends = [("r", {"x": xr}), ("l", {"x": xl}), ("c", {"c": other})]
    for label, where in gain_sends:
        send(gain, gbuf.at[x, c], ("gain", label), **where)
    spread.from_left(0)
    spread.from_right(0)
    spread.from_right(1)
    spread.from_left(1)
    arrived(gbuf.at[xl, c], ("gain", "r"), x=xr)
    send(gbuf.at[xl, c], gbuf.at[xl, c], ("gain", "rf"), x=xr)
    send(gbuf.at[xl, c], gbuf.at[xl, c], ("gain", "rc"), c=other)
    arrived(gbuf.at[xr, c], ("gain", "l"), x=xl)
    send(gbuf.at[xr, c], gbuf.at[xr, c], ("gain", "lc"), c=other)
    forward_y(weight_slot("k"), "wk")
    spread.from_far(0)
    spread.from_far(1)
    arrived(gbuf.at[xf, c], ("gain", "rf"), x=xr)
    send(gbuf.at[xf, c], gbuf.at[xf, c], ("gain", "fc"), c=other)
    spread.pass_on(0)
    spread.pass_on(1)
    gain_copy.wait()
    arrived(gbuf.at[x, other], ("gain", "c"), c=other)
    arrived(gbuf.at[xl, other], ("gain", "rc"), c=other)
    arrived(gbuf.at[xr, other], ("gain", "lc"), c=other)
    arrived(gbuf.at[xf, other], ("gain", "fc"), c=other)
    process(z, c, z, True)
    forward_y(weight_slot("v"), "wv")
    loads["q"].wait()
    gather_y(weight_slot("q"), "wq")
    for which, owner in (("zr", zl), ("zl", zr)):
        for h in range(2):
            spread.beside(which, h)
        process(4 + owner, c, owner, True)
    spread.paired(z, "own")
    process(8 + z, other, z, False)
    for h in range(2):
        spread.opposite(h)
    process(4 + zf, c, zf, True)
    for label, owner in (("zr", zl), ("zl", zr), ("zf", zf)):
        spread.paired(owner, label)
        process(8 + owner, other, owner, False)
    for t in range(4):
        s = jnp.sum(ssq[t].T, axis=0, keepdims=True)
        sqs[z, t] = jnp.broadcast_to(s, (8, block))
    for where, label in ((zr, 1), (zl, 3), (zf, 2)):
        send(sqs.at[z], sqs.at[z], ("sq", label), z=where)

    cw = wk.shape[1]

    def lower(ref):
        return ref.at[pl.ds(0, 2 * block)]

    def upper(ref):
        return ref.at[pl.ds(2 * block, 2 * block)]

    def project(name):
        j = order[name]
        width = xs.shape[3]
        tokens = 4 * block

        @pl.loop(0, cw // 256)
        def _(n):
            cols = pl.ds(pl.multiple_of(n * 256, 256), 256)
            w0 = wg[j, 0:2, :, cols].reshape(width, 256)
            w1 = wg[j, 2:4, :, cols].reshape(width, 256)
            left0 = xs[0].reshape(tokens, width)
            left1 = xs[1].reshape(tokens, width)
            acc = jnp.dot(left0, w0, preferred_element_type=F32)
            acc = acc + jnp.dot(left1, w1, preferred_element_type=F32)
            pbuf[j, 2 * n] = acc[:, :HD].astype(BF)
            pbuf[j, 2 * n + 1] = acc[:, HD:].astype(BF)

    def scatter(name):
        j = order[name]
        send(lower(pbuf.at[j, zf]), tr.at[j, 0], (name, "ta"), z=zr)
        send(upper(pbuf.at[j, zf]), tr.at[j, 1], (name, "tb"), z=zl)
        send(upper(pbuf.at[j, zr]), upper(fin.at[j, 0]), (name, "a1"), z=zr)
        send(lower(pbuf.at[j, zl]), lower(fin.at[j, 1]), (name, "b0"), z=zl)

    def relay(name):
        j = order[name]
        lo, hi = pl.ds(0, 2 * block), pl.ds(2 * block, 2 * block)
        arrived(tr.at[j, 0], (name, "ta"), z=zr)
        pbuf[j, zr, lo, :] = (pbuf[j, zr, lo, :].astype(F32) + tr[j, 0].astype(F32)).astype(BF)
        send(lower(pbuf.at[j, zr]), lower(fin.at[j, 0]), (name, "a0"), z=zr)
        arrived(tr.at[j, 1], (name, "tb"), z=zl)
        pbuf[j, zl, hi, :] = (pbuf[j, zl, hi, :].astype(F32) + tr[j, 1].astype(F32)).astype(BF)
        send(upper(pbuf.at[j, zl]), upper(fin.at[j, 1]), (name, "b1"), z=zl)

    def reduced(name):
        j = order[name]
        arrived(upper(fin.at[j, 0]), (name, "a1"), z=zr)
        arrived(lower(fin.at[j, 1]), (name, "b0"), z=zl)
        arrived(lower(fin.at[j, 0]), (name, "a0"), z=zr)
        arrived(upper(fin.at[j, 1]), (name, "b1"), z=zl)

    def total_of(name, t):
        j = order[name]
        r = pl.ds(t * block, block)
        total = pbuf[j, z, r, :].astype(F32) + fin[j, 0, r, :].astype(F32) + fin[j, 1, r, :].astype(F32)
        return total * rsc[r, :]

    def rotated(v, t):
        bases = tables[:16, :]
        here = lax.broadcasted_iota(jnp.int32, bases.shape, 0) == 4 * t + y
        base = jnp.sum(jnp.where(here, bases, 0.0), axis=0, keepdims=True)
        ca, sa = base[:, :HD], base[:, HD:]
        ci, si = tables[16:, :HD], tables[16:, HD:]
        cos = ca * ci - sa * si
        sin = sa * ci + ca * si
        lane = lax.broadcasted_iota(jnp.int32, (block, HD), 1)
        signed = jnp.where(lane < HD // 2, -sin, sin)
        return v * cos + pltpu.roll(v, HD // 2, axis=1) * signed

    finish_y(weight_slot("k"), "wk")
    project("k")
    scatter("k")
    finish_y(weight_slot("v"), "wv")
    project("v")
    relay("k")
    scatter("v")

    for where, label in ((zr, 1), (zl, 3), (zf, 2)):
        src = {1: zl, 3: zr, 2: zf}[label]
        arrived(sqs.at[src], ("sq", label), z=where)
    for t in range(4):
        s = sqs[0, t] + sqs[1, t] + sqs[2, t] + sqs[3, t]
        factor = lax.rsqrt(s / features + EPS)
        rsc[pl.ds(t * block, block), :] = jnp.broadcast_to(factor[0:1, :], (HD, block)).T

    def kv_slot(which):
        def slot(owner, part):
            ref = kvg.at[which]
            return ref.at[:, owner] if part is None else ref.at[pl.ds(2 * part, 2), owner]
        return slot

    def out_slot(owner, part):
        ref = wog.at[owner]
        count = wout.shape[0] // 2
        return ref if part is None else ref.at[pl.ds(part * count, count)]

    forward_y(weight_slot("q"), "wq")
    reduced("k")
    for t in range(4):
        kvg[0, t, y] = rotated(total_of("k", t), t).astype(BF)
    gather_y(kv_slot(0), "k")
    relay("v")
    finish_y(weight_slot("q"), "wq")
    project("q")
    scatter("q")
    reduced("v")
    for t in range(4):
        kvg[1, t, y] = total_of("v", t).astype(BF)
    gather_y(kv_slot(1), "v")
    relay("q")
    forward_y(kv_slot(0), "k")
    forward_y(kv_slot(1), "v")
    loads["o"].wait()
    gather_y(out_slot, "wo")
    reduced("q")
    for t in range(4):
        qbuf[t] = rotated(total_of("q", t), t).astype(BF)
    finish_y(kv_slot(0), "k")
    finish_y(kv_slot(1), "v")

    factor = math.log2(math.e) / math.sqrt(HD)
    span = 4 * block

    def keys(which, kb):
        return kvg[which, kb].reshape(span, HD)

    heads_base = [ids("c2", k) for k in range(4)][0]

    def head_copy(src, dst, target, source):
        return pltpu.make_async_remote_copy(
            src_ref=src, dst_ref=dst, send_sem=send_sem.at[heads_base + target],
            recv_sem=recv_sem.at[heads_base + source], device_id={"z": target}, device_id_type=MESH,
        )

    def context_sends(t):
        mine = cbig.at[x, pl.ds(t * block, block)]

        @pl.when(z != t)
        def _():
            head_copy(mine, ctxs.at[z], t, z).start()

        @pl.when(z == t)
        def _():
            ctxs[z] = cbig[x, pl.ds(t * block, block), :]

    around = Spread("c", cbig, ctransit)
    for t in range(4):
        q = qbuf[t]

        def score(kb, peak):
            s = lax.dot_general(q, keys(0, kb), (((1,), (1,)), ((), ())), preferred_element_type=F32)
            sbuf[kb] = s
            return jnp.maximum(peak, jnp.max(s, axis=1, keepdims=True))

        peak = jnp.full((block, 1), -1e30, F32)
        if t > 0:
            peak = lax.fori_loop(0, t, score, peak)
        s = lax.dot_general(q, keys(0, t), (((1,), (1,)), ((), ())), preferred_element_type=F32)
        row = lax.broadcasted_iota(jnp.int32, (block, span), 0) + y * block
        col = lax.broadcasted_iota(jnp.int32, (block, span), 1)
        s = jnp.where(col <= row, s, -jnp.inf)
        sbuf[t] = s
        peak = jnp.maximum(peak, jnp.max(s, axis=1, keepdims=True))

        def weigh(kb, carry):
            total, acc = carry
            p = jnp.exp2((sbuf[kb] - peak) * factor)
            total = total + jnp.sum(p, axis=1, keepdims=True)
            acc = acc + jnp.dot(p.astype(BF), keys(1, kb), preferred_element_type=F32)
            return total, acc

        total, acc = lax.fori_loop(
            0, t + 1, weigh, (jnp.zeros((block, 1), F32), jnp.zeros((block, HD), F32))
        )
        cbig[x, pl.ds(t * block, block), :] = (acc / total).astype(BF)
        if t % 2 == 1:
            around.own(t // 2)
        context_sends(t)
        if t == 2:
            around.from_left(0)
            around.from_right(0)

    around.from_right(1)
    around.from_left(1)
    around.from_far(0)
    around.from_far(1)
    around.pass_on(0)
    around.pass_on(1)
    forward_y(out_slot, "wo")
    for which in ("zr", "zl"):
        for h in range(2):
            around.beside(which, h)
    for h in range(2):
        around.opposite(h)

    for h in range(4):
        @pl.when(z != h)
        def _():
            copy = head_copy(ctxs.at[h], ctxs.at[h], h, h)
            copy.wait_send()
            copy.wait_recv()

    for h in range(4):
        ctx_out[:, h * HD:(h + 1) * HD] = ctxs[h]

    finish_y(out_slot, "wo")
    for label, owner in (("own", z), ("zr", zl), ("zl", zr), ("zf", zf)):
        around.paired(owner, label)

    def out_product(d):
        r = pl.ds(pl.multiple_of(d * block, block), block)
        slots = [
            jnp.where(c == p, jnp.where(z == k, k, 4 + k), 8 + k) for p in range(2) for k in range(4)
        ]
        left = jnp.concatenate([cbig[slot, r, :] for slot in slots], axis=1)
        right = wog[...].reshape(left.shape[1], wog.shape[2])
        return jnp.dot(left, right, preferred_element_type=F32)

    def first(ref):
        return ref.at[pl.ds(0, half)]

    def second(ref):
        return ref.at[pl.ds(half, half)]

    op[zf] = out_product(zf).astype(BF)
    send(first(op.at[zf]), otr.at[0], ("o", "ta"), z=zr)
    send(second(op.at[zf]), otr.at[1], ("o", "tb"), z=zl)
    op[zr] = out_product(zr).astype(BF)
    send(second(op.at[zr]), second(ofin.at[0]), ("o", "a1"), z=zr)
    op[zl] = out_product(zl).astype(BF)
    send(first(op.at[zl]), first(ofin.at[1]), ("o", "b0"), z=zl)
    lo, hi = pl.ds(0, half), pl.ds(half, half)
    arrived(otr.at[0], ("o", "ta"), z=zr)
    op[zr, lo, :] = (op[zr, lo, :].astype(F32) + otr[0].astype(F32)).astype(BF)
    send(first(op.at[zr]), first(ofin.at[0]), ("o", "a0"), z=zr)
    arrived(otr.at[1], ("o", "tb"), z=zl)
    op[zl, hi, :] = (op[zl, hi, :].astype(F32) + otr[1].astype(F32)).astype(BF)
    send(second(op.at[zl]), second(ofin.at[1]), ("o", "b1"), z=zl)
    oacc = big[x].astype(F32) + out_product(z)
    arrived(second(ofin.at[0]), ("o", "a1"), z=zr)
    arrived(first(ofin.at[1]), ("o", "b0"), z=zl)
    arrived(first(ofin.at[0]), ("o", "a0"), z=zr)
    arrived(second(ofin.at[1]), ("o", "b1"), z=zl)
    layer_out[...] = (oacc + ofin[0].astype(F32) + ofin[1].astype(F32)).astype(BF)
    for copy in sends:
        copy.wait_send()


def on_device(hidden, norm_gain, w_query, w_key, w_value, w_out):
    block, width = hidden.shape
    wrows, cw = w_query.shape
    orows, ow = w_out.shape
    features = 8 * width
    tables = jnp.asarray(rotary_tables(block, 16))
    vmem = pl.BlockSpec(memory_space=pltpu.VMEM)

    def body(*refs):
        kernel(features, *refs)

    return pl.pallas_call(
        body,
        out_shape=(
            jax.ShapeDtypeStruct((block, cw), BF),
            jax.ShapeDtypeStruct((block, ow), BF),
        ),
        in_specs=[pl.BlockSpec(memory_space=pl.ANY)] * 5 + [vmem] * 2,
        out_specs=(vmem, vmem),
        scratch_shapes=[
            pltpu.VMEM((12, block, width), BF),
            pltpu.VMEM((2, block // 2, width), BF),
            pltpu.VMEM((4, 2, 1, width), BF),
            pltpu.VMEM((2, 4, block, width), BF),
            pltpu.VMEM((4, block, HD), F32),
            pltpu.VMEM((4, 4, 8, block), F32),
            pltpu.VMEM((4 * block, HD), F32),
            pltpu.VMEM((3, 4, wrows, cw), BF),
            pltpu.VMEM((3, 4, 4 * block, HD), BF),
            pltpu.VMEM((3, 2, 2 * block, HD), BF),
            pltpu.VMEM((3, 2, 4 * block, HD), BF),
            pltpu.VMEM((2, 4, 4, block, HD), BF),
            pltpu.VMEM((4, block, HD), BF),
            pltpu.VMEM((4, block, 4 * block), F32),
            pltpu.VMEM((12, 4 * block, HD), BF),
            pltpu.VMEM((2, 2 * block, HD), BF),
            pltpu.VMEM((4, block, HD), BF),
            pltpu.VMEM((4, orows, ow), BF),
            pltpu.VMEM((4, block, ow), BF),
            pltpu.VMEM((2, block // 2, ow), BF),
            pltpu.VMEM((2, block, ow), BF),
            pltpu.SemaphoreType.DMA((N_MESSAGES,)),
            pltpu.SemaphoreType.DMA((N_MESSAGES,)),
            pltpu.SemaphoreType.DMA((N_MESSAGES,)),
        ],
        compiler_params=pltpu.CompilerParams(
            collective_id=0, has_side_effects=True, vmem_limit_bytes=62 * 1024 * 1024
        ),
    )(hidden, w_query, w_key, w_value, w_out, norm_gain.reshape(1, width), tables)


def solution(mesh):
    cube = Mesh(mesh.devices.reshape(4, 4, 4, 2), ("z", "y", "x", "c"))
    rows, cols = ("z", "y"), ("x", "c")
    both = P(rows, cols)
    return jax.shard_map(
        on_device,
        mesh=cube,
        in_specs=(both, P(cols), both, both, both, both),
        out_specs=(both, both),
        check_vma=False,
    )
```

```python
import math

import jax
import jax.numpy as jnp
import numpy as np
from jax import lax
from jax.experimental import pallas as pl
from jax.experimental.pallas import tpu as pltpu
from jax.sharding import Mesh, PartitionSpec as P

HD = 128
EPS = 1e-5
MESH = pl.DeviceIdType.MESH
BF = jnp.bfloat16
F32 = jnp.float32


def rotary_tables(block, blocks):
    freqs = np.exp(-math.log(10000.0) * 2.0 * np.arange(HD // 2) / HD)
    freqs = np.concatenate([freqs, freqs])[None, :]
    base = (np.arange(blocks) * block)[:, None] * freqs
    rows = np.arange(block)[:, None] * freqs
    angles = np.concatenate([base, rows], axis=0)
    return np.concatenate([np.cos(angles), np.sin(angles)], axis=1).astype(np.float32)


class Ids:
    def __init__(self):
        self.table = {}

    def __call__(self, *name):
        return self.table.setdefault(name, len(self.table))


N_MESSAGES = 160


def kernel(
    features, hidden, wq, wk, wv, wout, gain, tables,
    ctx_out, layer_out,
    big, transit, gbuf, xs, ssq, sqs, rsc, wg, pbuf, tr, fin, kvg, qbuf, sbuf,
    probs, cown, cx, ctxs, wog, op, otr, ofin, oacc, lout, send_sem, recv_sem, local_sem,
):
    z, y, x, c = (lax.axis_index(n) for n in ("z", "y", "x", "c"))
    zr, zl, zf = (lax.rem(z + k, 4) for k in (1, 3, 2))
    yr, yl, yf = (lax.rem(y + k, 4) for k in (1, 3, 2))
    xr, xl, xf = (lax.rem(x + k, 4) for k in (1, 3, 2))
    other = 1 - c
    block = hidden.shape[0]
    half = block // 2
    ids = Ids()
    sends = []

    def message(src, dst, name, **where):
        i = ids(*name)
        return pltpu.make_async_remote_copy(
            src_ref=src, dst_ref=dst, send_sem=send_sem.at[i], recv_sem=recv_sem.at[i],
            device_id=where, device_id_type=MESH,
        )

    def send(src, dst, name, **where):
        copy = message(src, dst, name, **where)
        copy.start()
        sends.append(copy)

    def arrived(dst, name, **where):
        message(dst, dst, name, **where).wait_recv()

    barrier = pltpu.get_barrier_semaphore()
    partners = [{"z": zr}, {"z": zl}, {"z": zf}, {"y": yr}, {"y": yl}, {"x": xr}, {"x": xl}, {"c": other}]
    for where in partners:
        pl.semaphore_signal(barrier, inc=1, device_id=where, device_id_type=MESH)

    def load(src, dst, name):
        copy = pltpu.make_async_copy(src, dst, local_sem.at[ids("load", name)])
        copy.start()
        return copy

    weights = {"k": wk, "v": wv, "q": wq}
    order = {"k": 0, "v": 1, "q": 2}
    loads = {"x": load(hidden, big.at[x], "x")}
    for name in "kvq":
        loads[name] = load(weights[name], wg.at[order[name], y], name)
    loads["o"] = load(wout, wog.at[z], "o")
    pl.semaphore_wait(barrier, len(partners))

    lines = {"y": (y, yr, yl, yf), "z": (z, zr, zl, zf)}

    def gather(axis, slot, name):
        me, right, left, _ = lines[axis]
        send(slot(me, None), slot(me, None), (name, "r"), **{axis: right})
        send(slot(me, None), slot(me, None), (name, "l"), **{axis: left})

    def forward(axis, slot, name):
        _, right, left, _ = lines[axis]
        arrived(slot(left, None), (name, "r"), **{axis: right})
        send(slot(left, 0), slot(left, 0), (name, "fr"), **{axis: right})
        arrived(slot(right, None), (name, "l"), **{axis: left})
        send(slot(right, 1), slot(right, 1), (name, "fl"), **{axis: left})

    def finish(axis, slot, name):
        _, right, left, far = lines[axis]
        arrived(slot(far, 0), (name, "fr"), **{axis: right})
        arrived(slot(far, 1), (name, "fl"), **{axis: left})

    def gather_y(slot, name):
        gather("y", slot, name)

    def forward_y(slot, name):
        forward("y", slot, name)

    def finish_y(slot, name):
        finish("y", slot, name)

    wrows = wk.shape[0]

    def weight_slot(name):
        def slot(owner, part):
            ref = wg.at[order[name], owner]
            return ref if part is None else ref.at[pl.ds(part * (wrows // 2), wrows // 2)]
        return slot

    class Spread:
        def __init__(self, name, buf, through):
            self.name, self.buf, self.through = name, buf, through
            self.rows = buf.shape[1] // 2

        def part(self, slot, h):
            return self.buf.at[slot, pl.ds(h * self.rows, self.rows)]

        def own(self, h):
            mine = self.part(x, h)
            send(mine, mine, (self.name, "xr", h), x=xr)
            send(mine, mine, (self.name, "xl", h), x=xl)
            self.onward(0, h)

        def pair(self, src_slot, owner, label, h):
            send(self.part(src_slot, h), self.part(8 + owner, h), (self.name, "pair", label, h), c=other)

        def onward(self, k, h):
            owner = lax.rem(x + k, 4)
            away = lax.rem(owner - z + 4, 4)
            src = self.part(owner, h)

            @pl.when(away == 0)
            def _():
                message(src, self.part(8 + z, h), (self.name, "pair", "own", h), c=other).start()

            @pl.when(away == 1)
            def _():
                message(src, self.part(4 + z, h), (self.name, "zr", h), z=zr).start()

            @pl.when(away == 3)
            def _():
                message(src, self.part(4 + z, h), (self.name, "zl", h), z=zl).start()

            @pl.when(away == 2)
            def _():
                to = {"z": zl} if h else {"z": zr}
                message(src, self.through.at[h], (self.name, "zz", h), **to).start()

            if k == 0:
                for label, where in (("zr", {"z": zr}), ("zl", {"z": zl}), ("zz", {"z": zl} if h else {"z": zr})):
                    sends.append(message(self.part(0, h), self.part(0, h), (self.name, label, h), **where))
                sends.append(message(self.part(0, h), self.part(0, h), (self.name, "pair", "own", h), c=other))

        def from_left(self, h):
            mine = self.part(xl, h)
            arrived(mine, (self.name, "xr", h), x=xr)
            if h == 0:
                send(mine, mine, (self.name, "xf", 0), x=xr)
            self.onward(3, h)

        def from_right(self, h):
            mine = self.part(xr, h)
            arrived(mine, (self.name, "xl", h), x=xl)
            if h == 1:
                send(mine, mine, (self.name, "xf", 1), x=xl)
            self.onward(1, h)

        def from_far(self, h):
            where = {"x": xl} if h else {"x": xr}
            arrived(self.part(xf, h), (self.name, "xf", h), **where)
            self.onward(2, h)

        def pass_on(self, h):
            where = {"z": zl} if h else {"z": zr}
            arrived(self.through.at[h], (self.name, "zz", h), **where)
            send(self.through.at[h], self.part(4 + (zr if h else zl), h), (self.name, "zf", h), **where)

        def beside(self, which, h):
            owner, where = (zl, {"z": zr}) if which == "zr" else (zr, {"z": zl})
            arrived(self.part(4 + owner, h), (self.name, which, h), **where)
            self.pair(4 + owner, owner, which, h)

        def opposite(self, h):
            where = {"z": zl} if h else {"z": zr}
            arrived(self.part(4 + zf, h), (self.name, "zf", h), **where)
            self.pair(4 + zf, zf, "zf", h)

        def paired(self, owner, label):
            for h in range(2):
                arrived(self.part(8 + owner, h), (self.name, "pair", label, h), c=other)

    def process(slot, plane, t, first):
        g = gbuf[z, plane].astype(F32)
        width = g.shape[1]

        @pl.loop(0, block // 32)
        def _(i):
            r = pl.ds(pl.multiple_of(i * 32, 32), 32)
            v = big[slot, r, :].astype(F32)
            xs[plane, t, r, :] = (v * g).astype(BF)
            sq = v * v
            total = sq[:, :HD]
            for k in range(1, width // HD):
                total = total + sq[:, k * HD:(k + 1) * HD]
            if first:
                ssq[t, r, :] = total
            else:
                ssq[t, r, :] = ssq[t, r, :] + total

    spread = Spread("h", big, transit)
    loads["x"].wait()
    for h in range(2):
        spread.own(h)
    loads["k"].wait()
    gather_y(weight_slot("k"), "wk")
    loads["v"].wait()
    gather_y(weight_slot("v"), "wv")
    gain_copy = pltpu.make_async_copy(gain, gbuf.at[x, c], local_sem.at[ids("gain")])
    gain_copy.start()
    gain_sends = [("r", {"x": xr}), ("l", {"x": xl}), ("c", {"c": other})]
    for label, where in gain_sends:
        send(gain, gbuf.at[x, c], ("gain", label), **where)
    spread.from_left(0)
    spread.from_right(0)
    spread.from_right(1)
    spread.from_left(1)
    arrived(gbuf.at[xl, c], ("gain", "r"), x=xr)
    send(gbuf.at[xl, c], gbuf.at[xl, c], ("gain", "rf"), x=xr)
    send(gbuf.at[xl, c], gbuf.at[xl, c], ("gain", "rc"), c=other)
    arrived(gbuf.at[xr, c], ("gain", "l"), x=xl)
    send(gbuf.at[xr, c], gbuf.at[xr, c], ("gain", "lc"), c=other)
    forward_y(weight_slot("k"), "wk")
    spread.from_far(0)
    spread.from_far(1)
    arrived(gbuf.at[xf, c], ("gain", "rf"), x=xr)
    send(gbuf.at[xf, c], gbuf.at[xf, c], ("gain", "fc"), c=other)
    spread.pass_on(0)
    spread.pass_on(1)
    gain_copy.wait()
    arrived(gbuf.at[x, other], ("gain", "c"), c=other)
    arrived(gbuf.at[xl, other], ("gain", "rc"), c=other)
    arrived(gbuf.at[xr, other], ("gain", "lc"), c=other)
    arrived(gbuf.at[xf, other], ("gain", "fc"), c=other)
    process(z, c, z, True)
    forward_y(weight_slot("v"), "wv")
    loads["q"].wait()
    gather_y(weight_slot("q"), "wq")
    for which, owner in (("zr", zl), ("zl", zr)):
        for h in range(2):
            spread.beside(which, h)
        process(4 + owner, c, owner, True)
    spread.paired(z, "own")
    process(8 + z, other, z, False)
    for h in range(2):
        spread.opposite(h)
    process(4 + zf, c, zf, True)
    for label, owner in (("zr", zl), ("zl", zr), ("zf", zf)):
        spread.paired(owner, label)
        process(8 + owner, other, owner, False)
    for t in range(4):
        s = jnp.sum(ssq[t].T, axis=0, keepdims=True)
        sqs[z, t] = jnp.broadcast_to(s, (8, block))
    for where, label in ((zr, 1), (zl, 3), (zf, 2)):
        send(sqs.at[z], sqs.at[z], ("sq", label), z=where)

    cw = wk.shape[1]

    def lower(ref):
        return ref.at[pl.ds(0, 2 * block)]

    def upper(ref):
        return ref.at[pl.ds(2 * block, 2 * block)]

    def project(name):
        j = order[name]
        width = xs.shape[3]
        tokens = 4 * block

        @pl.loop(0, cw // 256)
        def _(n):
            cols = pl.ds(pl.multiple_of(n * 256, 256), 256)
            w0 = wg[j, 0:2, :, cols].reshape(width, 256)
            w1 = wg[j, 2:4, :, cols].reshape(width, 256)
            left0 = xs[0].reshape(tokens, width)
            left1 = xs[1].reshape(tokens, width)
            acc = jnp.dot(left0, w0, preferred_element_type=F32)
            acc = acc + jnp.dot(left1, w1, preferred_element_type=F32)
            pbuf[j, 2 * n] = acc[:, :HD].astype(BF)
            pbuf[j, 2 * n + 1] = acc[:, HD:].astype(BF)

    def scatter(name):
        j = order[name]
        send(lower(pbuf.at[j, zf]), tr.at[j, 0], (name, "ta"), z=zr)
        send(upper(pbuf.at[j, zf]), tr.at[j, 1], (name, "tb"), z=zl)
        send(upper(pbuf.at[j, zr]), upper(fin.at[j, 0]), (name, "a1"), z=zr)
        send(lower(pbuf.at[j, zl]), lower(fin.at[j, 1]), (name, "b0"), z=zl)

    def relay(name):
        j = order[name]
        lo, hi = pl.ds(0, 2 * block), pl.ds(2 * block, 2 * block)
        arrived(tr.at[j, 0], (name, "ta"), z=zr)
        pbuf[j, zr, lo, :] = (pbuf[j, zr, lo, :].astype(F32) + tr[j, 0].astype(F32)).astype(BF)
        send(lower(pbuf.at[j, zr]), lower(fin.at[j, 0]), (name, "a0"), z=zr)
        arrived(tr.at[j, 1], (name, "tb"), z=zl)
        pbuf[j, zl, hi, :] = (pbuf[j, zl, hi, :].astype(F32) + tr[j, 1].astype(F32)).astype(BF)
        send(upper(pbuf.at[j, zl]), upper(fin.at[j, 1]), (name, "b1"), z=zl)

    def reduced(name):
        j = order[name]
        arrived(upper(fin.at[j, 0]), (name, "a1"), z=zr)
        arrived(lower(fin.at[j, 1]), (name, "b0"), z=zl)
        arrived(lower(fin.at[j, 0]), (name, "a0"), z=zr)
        arrived(upper(fin.at[j, 1]), (name, "b1"), z=zl)

    def total_of(name, t):
        j = order[name]
        r = pl.ds(t * block, block)
        total = pbuf[j, z, r, :].astype(F32) + fin[j, 0, r, :].astype(F32) + fin[j, 1, r, :].astype(F32)
        return total * rsc[r, :]

    def rotated(v, t):
        bases = tables[:16, :]
        here = lax.broadcasted_iota(jnp.int32, bases.shape, 0) == 4 * t + y
        base = jnp.sum(jnp.where(here, bases, 0.0), axis=0, keepdims=True)
        ca, sa = base[:, :HD], base[:, HD:]
        ci, si = tables[16:, :HD], tables[16:, HD:]
        cos = ca * ci - sa * si
        sin = sa * ci + ca * si
        lane = lax.broadcasted_iota(jnp.int32, (block, HD), 1)
        signed = jnp.where(lane < HD // 2, -sin, sin)
        return v * cos + pltpu.roll(v, HD // 2, axis=1) * signed

    finish_y(weight_slot("k"), "wk")
    project("k")
    scatter("k")
    finish_y(weight_slot("v"), "wv")
    project("v")
    relay("k")
    scatter("v")

    for where, label in ((zr, 1), (zl, 3), (zf, 2)):
        src = {1: zl, 3: zr, 2: zf}[label]
        arrived(sqs.at[src], ("sq", label), z=where)
    for t in range(4):
        s = sqs[0, t] + sqs[1, t] + sqs[2, t] + sqs[3, t]
        factor = lax.rsqrt(s / features + EPS)
        rsc[pl.ds(t * block, block), :] = jnp.broadcast_to(factor[0:1, :], (HD, block)).T

    def kv_slot(which):
        def slot(owner, part):
            ref = kvg.at[which]
            return ref.at[:, owner] if part is None else ref.at[pl.ds(2 * part, 2), owner]
        return slot

    def out_slot(owner, part):
        ref = wog.at[owner]
        count = wout.shape[0] // 2
        return ref if part is None else ref.at[pl.ds(part * count, count)]

    forward_y(weight_slot("q"), "wq")
    reduced("k")
    for t in range(4):
        kvg[0, t, y] = rotated(total_of("k", t), t).astype(BF)
    gather_y(kv_slot(0), "k")
    relay("v")
    finish_y(weight_slot("q"), "wq")
    project("q")
    scatter("q")
    reduced("v")
    for t in range(4):
        kvg[1, t, y] = total_of("v", t).astype(BF)
    gather_y(kv_slot(1), "v")
    relay("q")
    loads["o"].wait()
    gather("z", out_slot, "wo")
    forward_y(kv_slot(0), "k")
    forward_y(kv_slot(1), "v")
    reduced("q")
    for t in range(4):
        qbuf[t] = rotated(total_of("q", t), t).astype(BF)
    finish_y(kv_slot(0), "k")

    factor = math.log2(math.e) / math.sqrt(HD)
    span = 4 * block

    def keys(which, kb):
        return kvg[which, kb].reshape(span, HD)

    def base_of(name):
        return [ids(name, k) for k in range(4)][0]

    def direct(src, dst, name, to, source, **where):
        first = base_of(name)
        return pltpu.make_async_remote_copy(
            src_ref=src, dst_ref=dst, send_sem=send_sem.at[first + to],
            recv_sem=recv_sem.at[first + source], device_id=where, device_id_type=MESH,
        )

    sums = []
    for t in range(4):
        q = qbuf[t]

        def score(kb, peak):
            s = lax.dot_general(q, keys(0, kb), (((1,), (1,)), ((), ())), preferred_element_type=F32)
            sbuf[kb] = s
            return jnp.maximum(peak, jnp.max(s, axis=1, keepdims=True))

        peak = jnp.full((block, 1), -1e30, F32)
        if t > 0:
            peak = lax.fori_loop(0, t, score, peak)
        s = lax.dot_general(q, keys(0, t), (((1,), (1,)), ((), ())), preferred_element_type=F32)
        row = lax.broadcasted_iota(jnp.int32, (block, span), 0) + y * block
        col = lax.broadcasted_iota(jnp.int32, (block, span), 1)
        s = jnp.where(col <= row, s, -jnp.inf)
        sbuf[t] = s
        peak = jnp.maximum(peak, jnp.max(s, axis=1, keepdims=True))
        place = t * (t + 1) // 2

        def weigh(kb, total):
            p = jnp.exp2((sbuf[kb] - peak) * factor)
            probs[place + kb] = p.astype(BF)
            return total + jnp.sum(p, axis=1, keepdims=True)

        sums.append(lax.fori_loop(0, t + 1, weigh, jnp.zeros((block, 1), F32)))

    to_y, to_c = 2 * c + z // 2, lax.rem(z, 2)
    from_z, from_c = 2 * lax.rem(y, 2), y // 2
    finish_y(kv_slot(1), "v")
    for t in range(4):
        place = t * (t + 1) // 2

        def add(kb, acc):
            return acc + jnp.dot(probs[place + kb], keys(1, kb), preferred_element_type=F32)

        acc = lax.fori_loop(0, t + 1, add, jnp.zeros((block, HD), F32))
        cown[t] = (acc / sums[t]).astype(BF)
        itself = jnp.logical_and(z == t, jnp.logical_and(to_y == y, to_c == c))

        @pl.when(jnp.logical_not(itself))
        def _():
            direct(cown.at[t], cx.at[to_c, x, y], "cd", t, y, z=t, y=to_y, c=to_c).start()

        @pl.when(itself)
        def _():
            cx[c, x, y] = cown[t]

    for t in range(4):
        @pl.when(z != t)
        def _():
            direct(cown.at[t], ctxs.at[z], "c2", t, z, z=t).start()

        @pl.when(z == t)
        def _():
            ctxs[z] = cown[t]

    forward("z", out_slot, "wo")

    def cx_part(plane, owner, h):
        return cx.at[plane, owner, pl.ds(2 * h, 2)]

    def cx_pair(owner, label, h):
        send(cx_part(c, owner, h), cx_part(c, owner, h), ("cp", label, h), c=other)

    for h in range(2):
        for source in (2 * h, 2 * h + 1):
            source_z = from_z + c
            itself = jnp.logical_and(source == y, jnp.logical_and(source_z == z, from_c == c))

            @pl.when(jnp.logical_not(itself))
            def _():
                direct(cx.at[c, x, source], cx.at[c, x, source], "cd", source, source, z=z).wait_recv()

        send(cx_part(c, x, h), cx_part(c, x, h), ("cr", h), x=xr)
        send(cx_part(c, x, h), cx_part(c, x, h), ("cl", h), x=xl)
        cx_pair(x, "own", h)
    for t in range(4):
        itself = jnp.logical_and(z == t, jnp.logical_and(to_y == y, to_c == c))

        @pl.when(jnp.logical_not(itself))
        def _():
            direct(cown.at[t], cown.at[t], "cd", t, t, z=z).wait_send()

    arrived(cx_part(c, xl, 0), ("cr", 0), x=xr)
    send(cx_part(c, xl, 0), cx_part(c, xl, 0), ("cf", 0), x=xr)
    cx_pair(xl, "left", 0)
    arrived(cx_part(c, xr, 0), ("cl", 0), x=xl)
    cx_pair(xr, "right", 0)
    arrived(cx_part(c, xr, 1), ("cl", 1), x=xl)
    send(cx_part(c, xr, 1), cx_part(c, xr, 1), ("cf", 1), x=xl)
    cx_pair(xr, "right", 1)
    arrived(cx_part(c, xl, 1), ("cr", 1), x=xr)
    cx_pair(xl, "left", 1)

    context_out = []
    for h in range(4):
        @pl.when(z != h)
        def _():
            copy = direct(ctxs.at[h], ctxs.at[h], "c2", h, h, z=h)
            copy.wait_send()
            copy.wait_recv()

        copy = pltpu.make_async_copy(
            ctxs.at[h], ctx_out.at[:, pl.ds(h * HD, HD)], local_sem.at[ids("ctx", h)]
        )
        copy.start()
        context_out.append(copy)

    finish("z", out_slot, "wo")
    arrived(cx_part(c, xf, 0), ("cf", 0), x=xr)
    cx_pair(xf, "far", 0)
    arrived(cx_part(c, xf, 1), ("cf", 1), x=xl)
    cx_pair(xf, "far", 1)
    for label, owner in (("own", x), ("left", xl), ("right", xr), ("far", xf)):
        for h in range(2):
            arrived(cx_part(other, owner, h), ("cp", label, h), c=other)

    def out_product(d):
        left = jnp.concatenate([cx[p, k, d] for k in range(4) for p in range(2)], axis=1)
        right = wog[...].reshape(left.shape[1], wog.shape[2])
        return jnp.dot(left, right, preferred_element_type=F32)

    def first(ref):
        return ref.at[pl.ds(0, half)]

    def second(ref):
        return ref.at[pl.ds(half, half)]

    op[yf] = out_product(yf).astype(BF)
    send(first(op.at[yf]), otr.at[0], ("o", "ta"), y=yr)
    send(second(op.at[yf]), otr.at[1], ("o", "tb"), y=yl)
    op[yr] = out_product(yr).astype(BF)
    send(second(op.at[yr]), second(ofin.at[0]), ("o", "a1"), y=yr)
    op[yl] = out_product(yl).astype(BF)
    send(first(op.at[yl]), first(ofin.at[1]), ("o", "b0"), y=yl)
    lo, hi = pl.ds(0, half), pl.ds(half, half)
    arrived(otr.at[0], ("o", "ta"), y=yr)
    op[yr, lo, :] = (op[yr, lo, :].astype(F32) + otr[0].astype(F32)).astype(BF)
    send(first(op.at[yr]), first(ofin.at[0]), ("o", "a0"), y=yr)
    arrived(otr.at[1], ("o", "tb"), y=yl)
    op[yl, hi, :] = (op[yl, hi, :].astype(F32) + otr[1].astype(F32)).astype(BF)
    send(second(op.at[yl]), second(ofin.at[1]), ("o", "b1"), y=yl)
    oacc[...] = big[x].astype(F32) + out_product(y)
    arrived(second(ofin.at[0]), ("o", "a1"), y=yr)
    arrived(first(ofin.at[1]), ("o", "b0"), y=yl)
    out_copies = []
    for h, side, name, where in ((0, 0, "a0", {"y": yr}), (1, 1, "b1", {"y": yl})):
        r = pl.ds(h * half, half)
        arrived(ofin.at[side, r], ("o", name), **where)
        lout[r, :] = (oacc[r, :] + ofin[0, r, :].astype(F32) + ofin[1, r, :].astype(F32)).astype(BF)
        copy = pltpu.make_async_copy(lout.at[r], layer_out.at[r], local_sem.at[ids("lout", h)])
        copy.start()
        out_copies.append(copy)
    for copy in sends:
        copy.wait_send()
    for copy in context_out + out_copies:
        copy.wait()


def on_device(hidden, norm_gain, w_query, w_key, w_value, w_out):
    block, width = hidden.shape
    wrows, cw = w_query.shape
    orows, ow = w_out.shape
    features = 8 * width
    tables = jnp.asarray(rotary_tables(block, 16))
    vmem = pl.BlockSpec(memory_space=pltpu.VMEM)

    def body(*refs):
        kernel(features, *refs)

    return pl.pallas_call(
        body,
        out_shape=(
            jax.ShapeDtypeStruct((block, cw), BF),
            jax.ShapeDtypeStruct((block, ow), BF),
        ),
        in_specs=[pl.BlockSpec(memory_space=pl.ANY)] * 5 + [vmem] * 2,
        out_specs=(pl.BlockSpec(memory_space=pl.ANY),) * 2,
        scratch_shapes=[
            pltpu.VMEM((12, block, width), BF),
            pltpu.VMEM((2, block // 2, width), BF),
            pltpu.VMEM((4, 2, 1, width), BF),
            pltpu.VMEM((2, 4, block, width), BF),
            pltpu.VMEM((4, block, HD), F32),
            pltpu.VMEM((4, 4, 8, block), F32),
            pltpu.VMEM((4 * block, HD), F32),
            pltpu.VMEM((3, 4, wrows, cw), BF),
            pltpu.VMEM((3, 4, 4 * block, HD), BF),
            pltpu.VMEM((3, 2, 2 * block, HD), BF),
            pltpu.VMEM((3, 2, 4 * block, HD), BF),
            pltpu.VMEM((2, 4, 4, block, HD), BF),
            pltpu.VMEM((4, block, HD), BF),
            pltpu.VMEM((4, block, 4 * block), F32),
            pltpu.VMEM((10, block, 4 * block), BF),
            pltpu.VMEM((4, block, HD), BF),
            pltpu.VMEM((2, 4, 4, block, HD), BF),
            pltpu.VMEM((4, block, HD), BF),
            pltpu.VMEM((4, orows, ow), BF),
            pltpu.VMEM((4, block, ow), BF),
            pltpu.VMEM((2, block // 2, ow), BF),
            pltpu.VMEM((2, block, ow), BF),
            pltpu.VMEM((block, ow), F32),
            pltpu.VMEM((block, ow), BF),
            pltpu.SemaphoreType.DMA((N_MESSAGES,)),
            pltpu.SemaphoreType.DMA((N_MESSAGES,)),
            pltpu.SemaphoreType.DMA((N_MESSAGES,)),
        ],
        compiler_params=pltpu.CompilerParams(
            collective_id=0, has_side_effects=True, vmem_limit_bytes=62 * 1024 * 1024
        ),
    )(hidden, w_query, w_key, w_value, w_out, norm_gain.reshape(1, width), tables)


def solution(mesh):
    cube = Mesh(mesh.devices.reshape(4, 4, 4, 2), ("z", "y", "x", "c"))
    rows, cols = ("z", "y"), ("x", "c")
    both = P(rows, cols)
    return jax.shard_map(
        on_device,
        mesh=cube,
        in_specs=(both, P(cols), both, both, both, both),
        out_specs=(both, both),
        check_vma=False,
    )
```

```python
import math

import jax
import jax.numpy as jnp
import numpy as np
from jax import lax
from jax.experimental import pallas as pl
from jax.experimental.pallas import tpu as pltpu
from jax.sharding import Mesh, PartitionSpec as P

HD = 128
EPS = 1e-5
MESH = pl.DeviceIdType.MESH
BF = jnp.bfloat16
F32 = jnp.float32


def rotary_tables(block, blocks):
    freqs = np.exp(-math.log(10000.0) * 2.0 * np.arange(HD // 2) / HD)
    freqs = np.concatenate([freqs, freqs])[None, :]
    base = (np.arange(blocks) * block)[:, None] * freqs
    rows = np.arange(block)[:, None] * freqs
    angles = np.concatenate([base, rows], axis=0)
    return np.concatenate([np.cos(angles), np.sin(angles)], axis=1).astype(np.float32)


class Ids:
    def __init__(self):
        self.table = {}

    def __call__(self, *name):
        return self.table.setdefault(name, len(self.table))


N_MESSAGES = 138
N_LOCAL = 14


def kernel(
    features, hidden, wq, wk, wv, wout, gain, tables,
    ctx_out, layer_out,
    big, transit, gbuf, xs, ssq, sqs, rsc, wg, pbuf, tr, fin, kvg, qbuf, sbuf,
    probs, cown, cx, ctxs, wog, lhs, op, otr, ofin, oacc, lout, send_sem, recv_sem, local_sem,
):
    z, y, x, c = (lax.axis_index(n) for n in ("z", "y", "x", "c"))
    zr, zl, zf = (lax.rem(z + k, 4) for k in (1, 3, 2))
    yr, yl, yf = (lax.rem(y + k, 4) for k in (1, 3, 2))
    xr, xl, xf = (lax.rem(x + k, 4) for k in (1, 3, 2))
    other = 1 - c
    block = hidden.shape[0]
    half = block // 2
    ids, local_ids = Ids(), Ids()
    sends = []

    def message(src, dst, name, **where):
        i = ids(*name)
        return pltpu.make_async_remote_copy(
            src_ref=src, dst_ref=dst, send_sem=send_sem.at[i], recv_sem=recv_sem.at[i],
            device_id=where, device_id_type=MESH,
        )

    def send(src, dst, name, **where):
        copy = message(src, dst, name, **where)
        copy.start()
        sends.append(copy)

    def arrived(dst, name, **where):
        message(dst, dst, name, **where).wait_recv()

    barrier = pltpu.get_barrier_semaphore()
    partners = [{"z": zr}, {"z": zl}, {"z": zf}, {"y": yr}, {"y": yl}, {"x": xr}, {"x": xl}, {"c": other}]
    for where in partners:
        pl.semaphore_signal(barrier, inc=1, device_id=where, device_id_type=MESH)

    def load(src, dst, name):
        copy = pltpu.make_async_copy(src, dst, local_sem.at[local_ids("load", name)])
        copy.start()
        return copy

    weights = {"k": wk, "v": wv, "q": wq}
    order = {"k": 0, "v": 1, "q": 2}
    loads = {"x": load(hidden, big.at[x], "x")}
    for name in "kvq":
        loads[name] = load(weights[name], wg.at[order[name], y], name)
    loads["o"] = load(wout, wog.at[z], "o")
    pl.semaphore_wait(barrier, len(partners))

    lines = {"y": (y, yr, yl, yf), "z": (z, zr, zl, zf)}

    def gather(axis, slot, name):
        me, right, left, _ = lines[axis]
        for h, side, to in ((0, "r", right), (1, "l", left), (1, "r", right), (0, "l", left)):
            send(slot(me, h), slot(me, h), (name, side, h), **{axis: to})

    def forward(axis, slot, name):
        _, right, left, _ = lines[axis]
        arrived(slot(left, 0), (name, "r", 0), **{axis: right})
        send(slot(left, 0), slot(left, 0), (name, "fr"), **{axis: right})
        arrived(slot(right, 1), (name, "l", 1), **{axis: left})
        send(slot(right, 1), slot(right, 1), (name, "fl"), **{axis: left})

    def finish(axis, slot, name):
        _, right, left, far = lines[axis]
        arrived(slot(left, 1), (name, "r", 1), **{axis: right})
        arrived(slot(right, 0), (name, "l", 0), **{axis: left})
        arrived(slot(far, 0), (name, "fr"), **{axis: right})
        arrived(slot(far, 1), (name, "fl"), **{axis: left})

    def gather_y(slot, name):
        gather("y", slot, name)

    def forward_y(slot, name):
        forward("y", slot, name)

    def finish_y(slot, name):
        finish("y", slot, name)

    wrows = wk.shape[0]

    def weight_slot(name):
        def slot(owner, part):
            ref = wg.at[order[name], owner]
            return ref if part is None else ref.at[pl.ds(part * (wrows // 2), wrows // 2)]
        return slot

    class Spread:
        def __init__(self, name, buf, through):
            self.name, self.buf, self.through = name, buf, through
            self.rows = buf.shape[1] // 2

        def part(self, slot, h):
            return self.buf.at[slot, pl.ds(h * self.rows, self.rows)]

        def own(self, h):
            mine = self.part(x, h)
            send(mine, mine, (self.name, "xr", h), x=xr)
            send(mine, mine, (self.name, "xl", h), x=xl)
            self.onward(0, h)

        def pair(self, src_slot, owner, label, h):
            send(self.part(src_slot, h), self.part(8 + owner, h), (self.name, "pair", label, h), c=other)

        def onward(self, k, h):
            owner = lax.rem(x + k, 4)
            away = lax.rem(owner - z + 4, 4)
            src = self.part(owner, h)

            @pl.when(away == 0)
            def _():
                message(src, self.part(8 + z, h), (self.name, "pair", "own", h), c=other).start()

            @pl.when(away == 1)
            def _():
                message(src, self.part(4 + z, h), (self.name, "zr", h), z=zr).start()

            @pl.when(away == 3)
            def _():
                message(src, self.part(4 + z, h), (self.name, "zl", h), z=zl).start()

            @pl.when(away == 2)
            def _():
                to = {"z": zl} if h else {"z": zr}
                message(src, self.through.at[h], (self.name, "zz", h), **to).start()

            if k == 0:
                for label, where in (("zr", {"z": zr}), ("zl", {"z": zl}), ("zz", {"z": zl} if h else {"z": zr})):
                    sends.append(message(self.part(0, h), self.part(0, h), (self.name, label, h), **where))
                sends.append(message(self.part(0, h), self.part(0, h), (self.name, "pair", "own", h), c=other))

        def from_left(self, h):
            mine = self.part(xl, h)
            arrived(mine, (self.name, "xr", h), x=xr)
            if h == 0:
                send(mine, mine, (self.name, "xf", 0), x=xr)
            self.onward(3, h)

        def from_right(self, h):
            mine = self.part(xr, h)
            arrived(mine, (self.name, "xl", h), x=xl)
            if h == 1:
                send(mine, mine, (self.name, "xf", 1), x=xl)
            self.onward(1, h)

        def from_far(self, h):
            where = {"x": xl} if h else {"x": xr}
            arrived(self.part(xf, h), (self.name, "xf", h), **where)
            self.onward(2, h)

        def pass_on(self, h):
            where = {"z": zl} if h else {"z": zr}
            arrived(self.through.at[h], (self.name, "zz", h), **where)
            send(self.through.at[h], self.part(4 + (zr if h else zl), h), (self.name, "zf", h), **where)

        def beside(self, which, h):
            owner, where = (zl, {"z": zr}) if which == "zr" else (zr, {"z": zl})
            arrived(self.part(4 + owner, h), (self.name, which, h), **where)
            self.pair(4 + owner, owner, which, h)

        def opposite(self, h):
            where = {"z": zl} if h else {"z": zr}
            arrived(self.part(4 + zf, h), (self.name, "zf", h), **where)
            self.pair(4 + zf, zf, "zf", h)

        def paired(self, owner, label):
            for h in range(2):
                arrived(self.part(8 + owner, h), (self.name, "pair", label, h), c=other)

    def process(slot, plane, t, first):
        g = gbuf[z, plane].astype(F32)
        width = g.shape[1]

        @pl.loop(0, block // 32)
        def _(i):
            r = pl.ds(pl.multiple_of(i * 32, 32), 32)
            v = big[slot, r, :].astype(F32)
            xs[plane, t, r, :] = (v * g).astype(BF)
            sq = v * v
            total = sq[:, :HD]
            for k in range(1, width // HD):
                total = total + sq[:, k * HD:(k + 1) * HD]
            if first:
                ssq[t, r, :] = total
            else:
                ssq[t, r, :] = ssq[t, r, :] + total

    spread = Spread("h", big, transit)
    loads["x"].wait()
    for h in range(2):
        spread.own(h)
    loads["k"].wait()
    gather_y(weight_slot("k"), "wk")
    loads["v"].wait()
    gather_y(weight_slot("v"), "wv")
    gain_copy = pltpu.make_async_copy(gain, gbuf.at[x, c], local_sem.at[local_ids("gain")])
    gain_copy.start()
    gain_sends = [("r", {"x": xr}), ("l", {"x": xl}), ("c", {"c": other})]
    for label, where in gain_sends:
        send(gain, gbuf.at[x, c], ("gain", label), **where)
    spread.from_left(0)
    spread.from_right(0)
    spread.from_right(1)
    spread.from_left(1)
    arrived(gbuf.at[xl, c], ("gain", "r"), x=xr)
    send(gbuf.at[xl, c], gbuf.at[xl, c], ("gain", "rf"), x=xr)
    send(gbuf.at[xl, c], gbuf.at[xl, c], ("gain", "rc"), c=other)
    arrived(gbuf.at[xr, c], ("gain", "l"), x=xl)
    send(gbuf.at[xr, c], gbuf.at[xr, c], ("gain", "lc"), c=other)
    forward_y(weight_slot("k"), "wk")
    spread.from_far(0)
    spread.from_far(1)
    arrived(gbuf.at[xf, c], ("gain", "rf"), x=xr)
    send(gbuf.at[xf, c], gbuf.at[xf, c], ("gain", "fc"), c=other)
    spread.pass_on(0)
    spread.pass_on(1)
    gain_copy.wait()
    arrived(gbuf.at[x, other], ("gain", "c"), c=other)
    arrived(gbuf.at[xl, other], ("gain", "rc"), c=other)
    arrived(gbuf.at[xr, other], ("gain", "lc"), c=other)
    arrived(gbuf.at[xf, other], ("gain", "fc"), c=other)
    process(z, c, z, True)
    forward_y(weight_slot("v"), "wv")
    loads["q"].wait()
    gather_y(weight_slot("q"), "wq")
    for which, owner in (("zr", zl), ("zl", zr)):
        for h in range(2):
            spread.beside(which, h)
        process(4 + owner, c, owner, True)
    spread.paired(z, "own")
    process(8 + z, other, z, False)
    for h in range(2):
        spread.opposite(h)
    process(4 + zf, c, zf, True)
    for label, owner in (("zr", zl), ("zl", zr), ("zf", zf)):
        spread.paired(owner, label)
        process(8 + owner, other, owner, False)
    for t in range(4):
        s = jnp.sum(ssq[t].T, axis=0, keepdims=True)
        sqs[z, t] = jnp.broadcast_to(s, (8, block))
    for where, label in ((zr, 1), (zl, 3), (zf, 2)):
        send(sqs.at[z], sqs.at[z], ("sq", label), z=where)

    cw = wk.shape[1]

    def lower(ref):
        return ref.at[pl.ds(0, 2 * block)]

    def upper(ref):
        return ref.at[pl.ds(2 * block, 2 * block)]

    def project(name):
        j = order[name]
        width = xs.shape[3]
        tokens = 4 * block

        @pl.loop(0, cw // 256)
        def _(n):
            cols = pl.ds(pl.multiple_of(n * 256, 256), 256)
            w0 = wg[j, 0:2, :, cols].reshape(width, 256)
            w1 = wg[j, 2:4, :, cols].reshape(width, 256)
            left0 = xs[0].reshape(tokens, width)
            left1 = xs[1].reshape(tokens, width)
            acc = jnp.dot(left0, w0, preferred_element_type=F32)
            acc = acc + jnp.dot(left1, w1, preferred_element_type=F32)
            pbuf[j, 2 * n] = acc[:, :HD].astype(BF)
            pbuf[j, 2 * n + 1] = acc[:, HD:].astype(BF)

    def scatter(name):
        j = order[name]
        send(lower(pbuf.at[j, zf]), tr.at[j, 0], (name, "ta"), z=zr)
        send(upper(pbuf.at[j, zf]), tr.at[j, 1], (name, "tb"), z=zl)
        send(upper(pbuf.at[j, zr]), upper(fin.at[j, 0]), (name, "a1"), z=zr)
        send(lower(pbuf.at[j, zl]), lower(fin.at[j, 1]), (name, "b0"), z=zl)

    def relay(name):
        j = order[name]
        lo, hi = pl.ds(0, 2 * block), pl.ds(2 * block, 2 * block)
        arrived(tr.at[j, 0], (name, "ta"), z=zr)
        pbuf[j, zr, lo, :] = (pbuf[j, zr, lo, :].astype(F32) + tr[j, 0].astype(F32)).astype(BF)
        send(lower(pbuf.at[j, zr]), lower(fin.at[j, 0]), (name, "a0"), z=zr)
        arrived(tr.at[j, 1], (name, "tb"), z=zl)
        pbuf[j, zl, hi, :] = (pbuf[j, zl, hi, :].astype(F32) + tr[j, 1].astype(F32)).astype(BF)
        send(upper(pbuf.at[j, zl]), upper(fin.at[j, 1]), (name, "b1"), z=zl)

    def reduced(name):
        j = order[name]
        arrived(upper(fin.at[j, 0]), (name, "a1"), z=zr)
        arrived(lower(fin.at[j, 1]), (name, "b0"), z=zl)
        arrived(lower(fin.at[j, 0]), (name, "a0"), z=zr)
        arrived(upper(fin.at[j, 1]), (name, "b1"), z=zl)

    def total_of(name, t):
        j = order[name]
        r = pl.ds(t * block, block)
        total = pbuf[j, z, r, :].astype(F32) + fin[j, 0, r, :].astype(F32) + fin[j, 1, r, :].astype(F32)
        return total * rsc[r, :]

    def rotated(v, t):
        bases = tables[:16, :]
        here = lax.broadcasted_iota(jnp.int32, bases.shape, 0) == 4 * t + y
        base = jnp.sum(jnp.where(here, bases, 0.0), axis=0, keepdims=True)
        ca, sa = base[:, :HD], base[:, HD:]
        ci, si = tables[16:, :HD], tables[16:, HD:]
        cos = ca * ci - sa * si
        sin = sa * ci + ca * si
        lane = lax.broadcasted_iota(jnp.int32, (block, HD), 1)
        signed = jnp.where(lane < HD // 2, -sin, sin)
        return v * cos + pltpu.roll(v, HD // 2, axis=1) * signed

    finish_y(weight_slot("k"), "wk")
    project("k")
    scatter("k")
    finish_y(weight_slot("v"), "wv")
    project("v")
    relay("k")
    scatter("v")

    for where, label in ((zr, 1), (zl, 3), (zf, 2)):
        src = {1: zl, 3: zr, 2: zf}[label]
        arrived(sqs.at[src], ("sq", label), z=where)
    for t in range(4):
        s = sqs[0, t] + sqs[1, t] + sqs[2, t] + sqs[3, t]
        factor = lax.rsqrt(s / features + EPS)
        rsc[pl.ds(t * block, block), :] = jnp.broadcast_to(factor[0:1, :], (HD, block)).T

    def kv_slot(which):
        def slot(owner, part):
            ref = kvg.at[which]
            return ref.at[:, owner] if part is None else ref.at[pl.ds(2 * part, 2), owner]
        return slot

    def out_slot(owner, part):
        ref = wog.at[owner]
        count = wout.shape[0] // 2
        return ref if part is None else ref.at[pl.ds(part * count, count)]

    forward_y(weight_slot("q"), "wq")
    reduced("k")
    for t in range(4):
        kvg[0, t, y] = rotated(total_of("k", t), t).astype(BF)
    gather_y(kv_slot(0), "k")
    relay("v")
    finish_y(weight_slot("q"), "wq")
    project("q")
    scatter("q")
    forward_y(kv_slot(0), "k")
    reduced("v")
    for t in range(4):
        kvg[1, t, y] = total_of("v", t).astype(BF)
    gather_y(kv_slot(1), "v")
    relay("q")
    loads["o"].wait()
    gather("z", out_slot, "wo")
    forward_y(kv_slot(1), "v")
    reduced("q")
    for t in range(4):
        qbuf[t] = rotated(total_of("q", t), t).astype(BF)
    finish_y(kv_slot(0), "k")

    factor = math.log2(math.e) / math.sqrt(HD)
    span = 4 * block

    def keys(which, kb):
        return kvg[which, kb].reshape(span, HD)

    def base_of(name):
        return [ids(*name, k) for k in range(4)][0]

    def direct(src, dst, name, to, source, **where):
        first = base_of(name)
        return pltpu.make_async_remote_copy(
            src_ref=src, dst_ref=dst, send_sem=send_sem.at[first + to],
            recv_sem=recv_sem.at[first + source], device_id=where, device_id_type=MESH,
        )

    to_y, to_c = 2 * c + z // 2, lax.rem(z, 2)
    from_z, from_c = 2 * lax.rem(y, 2) + c, y // 2

    def rows_of(part):
        return pl.ds(part * half, half)

    def score_rows(part):
        mine = rows_of(part)
        sums = []
        for t in range(4):
            q = qbuf[t, mine, :]

            def score(kb, peak):
                s = lax.dot_general(q, keys(0, kb), (((1,), (1,)), ((), ())), preferred_element_type=F32)
                sbuf[kb] = s
                return jnp.maximum(peak, jnp.max(s, axis=1, keepdims=True))

            peak = jnp.full((half, 1), -1e30, F32)
            if t > 0:
                peak = lax.fori_loop(0, t, score, peak)
            s = lax.dot_general(q, keys(0, t), (((1,), (1,)), ((), ())), preferred_element_type=F32)
            row = lax.broadcasted_iota(jnp.int32, (half, span), 0) + (y * block + part * half)
            col = lax.broadcasted_iota(jnp.int32, (half, span), 1)
            s = jnp.where(col <= row, s, -jnp.inf)
            sbuf[t] = s
            peak = jnp.maximum(peak, jnp.max(s, axis=1, keepdims=True))
            place = t * (t + 1) // 2

            def weigh(kb, total):
                p = jnp.exp2((sbuf[kb] - peak) * factor)
                probs[place + kb] = p.astype(BF)
                return total + jnp.sum(p, axis=1, keepdims=True)

            sums.append(lax.fori_loop(0, t + 1, weigh, jnp.zeros((half, 1), F32)))
        return sums

    def context_rows(part, sums):
        mine = rows_of(part)
        for t in range(4):
            place = t * (t + 1) // 2

            def add(kb, acc):
                return acc + jnp.dot(probs[place + kb], keys(1, kb), preferred_element_type=F32)

            acc = lax.fori_loop(0, t + 1, add, jnp.zeros((half, HD), F32))
            cown[t, mine, :] = (acc / sums[t]).astype(BF)
            itself = jnp.logical_and(z == t, jnp.logical_and(to_y == y, to_c == c))

            @pl.when(jnp.logical_not(itself))
            def _():
                direct(
                    cown.at[t, mine], cx.at[to_c, x, y, mine], ("cd", part), t, y,
                    z=t, y=to_y, c=to_c,
                ).start()

            @pl.when(itself)
            def _():
                cx[c, x, y, mine, :] = cown[t, mine, :]

    def cx_part(plane, owner, part, h):
        return cx.at[plane, owner, pl.ds(2 * h, 2), rows_of(part)]

    def cx_pair(owner, label, part, h):
        mine = cx_part(c, owner, part, h)
        send(mine, mine, ("cp", label, part, h), c=other)

    def context_around(part):
        mine = rows_of(part)
        for source in range(4):
            itself = jnp.logical_and(source == y, jnp.logical_and(from_z == z, from_c == c))

            @pl.when(jnp.logical_not(itself))
            def _():
                ref = cx.at[c, x, source, mine]
                direct(ref, ref, ("cd", part), source, source, z=z).wait_recv()

        for h, side, where in ((0, "cr", {"x": xr}), (1, "cl", {"x": xl}), (1, "cr", {"x": xr}), (0, "cl", {"x": xl})):
            send(cx_part(c, x, part, h), cx_part(c, x, part, h), (side, part, h), **where)
        for h in range(2):
            cx_pair(x, "own", part, h)

    def context_beside(part):
        left, right = cx_part(c, xl, part, 0), cx_part(c, xr, part, 1)
        arrived(left, ("cr", part, 0), x=xr)
        send(left, left, ("cf", part, 0), x=xr)
        cx_pair(xl, "left", part, 0)
        arrived(right, ("cl", part, 1), x=xl)
        send(right, right, ("cf", part, 1), x=xl)
        cx_pair(xr, "right", part, 1)

    def context_far(part):
        arrived(cx_part(c, xl, part, 1), ("cr", part, 1), x=xr)
        cx_pair(xl, "left", part, 1)
        arrived(cx_part(c, xr, part, 0), ("cl", part, 0), x=xl)
        cx_pair(xr, "right", part, 0)
        arrived(cx_part(c, xf, part, 0), ("cf", part, 0), x=xr)
        cx_pair(xf, "far", part, 0)
        arrived(cx_part(c, xf, part, 1), ("cf", part, 1), x=xl)
        cx_pair(xf, "far", part, 1)

    targets = (yf, yr, yl, y)

    def out_product(part):
        mine = rows_of(part)
        for label, owner in (("own", x), ("left", xl), ("right", xr), ("far", xf)):
            for h in range(2):
                arrived(cx_part(other, owner, part, h), ("cp", label, part, h), c=other)
        for i, d in enumerate(targets):
            for k in range(4):
                for p in range(2):
                    lhs[i * half:(i + 1) * half, (2 * k + p) * HD:(2 * k + p + 1) * HD] = cx[p, k, d, mine, :]
        depth = lhs.shape[1]

        @pl.loop(0, wog.shape[2] // 256)
        def _(n):
            cols = pl.ds(pl.multiple_of(n * 256, 256), 256)
            acc = jnp.dot(lhs[...], wog[:, :, cols].reshape(depth, 256), preferred_element_type=F32)
            for i in range(3):
                op[targets[i], mine, cols] = acc[i * half:(i + 1) * half].astype(BF)
            oacc[mine, cols] = acc[3 * half:]

    quarter = half // 2

    def piece(part, h):
        return pl.ds(part * half + h * quarter, quarter)

    def out_scatter(part):
        send(op.at[yf, piece(part, 0)], otr.at[part, 0], ("o", part, "ta"), y=yr)
        send(op.at[yf, piece(part, 1)], otr.at[part, 1], ("o", part, "tb"), y=yl)
        send(op.at[yr, piece(part, 1)], ofin.at[0, piece(part, 1)], ("o", part, "a1"), y=yr)
        send(op.at[yl, piece(part, 0)], ofin.at[1, piece(part, 0)], ("o", part, "b0"), y=yl)

    def out_relay(part):
        for h, to, where, came, name in ((0, yr, {"y": yr}, "ta", "a0"), (1, yl, {"y": yl}, "tb", "b1")):
            r = piece(part, h)
            arrived(otr.at[part, h], ("o", part, came), **where)
            op[to, r, :] = (op[to, r, :].astype(F32) + otr[part, h].astype(F32)).astype(BF)
            send(op.at[to, r], ofin.at[h, r], ("o", part, name), **where)

    copies_out = []

    def out_finish(part):
        arrived(ofin.at[0, piece(part, 1)], ("o", part, "a1"), y=yr)
        arrived(ofin.at[1, piece(part, 0)], ("o", part, "b0"), y=yl)
        for h, name, where in ((0, "a0", {"y": yr}), (1, "b1", {"y": yl})):
            r = piece(part, h)
            arrived(ofin.at[h, r], ("o", part, name), **where)
            total = big[x, r, :].astype(F32) + oacc[r, :]
            lout[r, :] = (total + ofin[0, r, :].astype(F32) + ofin[1, r, :].astype(F32)).astype(BF)
            copy = pltpu.make_async_copy(lout.at[r], layer_out.at[r], local_sem.at[local_ids("lout", part, h)])
            copy.start()
            copies_out.append(copy)

    sums = score_rows(0)
    finish_y(kv_slot(1), "v")
    context_rows(0, sums)
    forward("z", out_slot, "wo")
    context_rows(1, score_rows(1))
    context_around(0)
    for t in range(4):
        @pl.when(z != t)
        def _():
            direct(cown.at[t], ctxs.at[z], ("c2",), t, z, z=t).start()

        @pl.when(z == t)
        def _():
            ctxs[z] = cown[t]

    context_beside(0)
    context_around(1)
    context_far(0)
    finish("z", out_slot, "wo")
    out_product(0)
    out_scatter(0)
    context_beside(1)
    context_far(1)
    out_relay(0)
    out_product(1)
    out_scatter(1)

    for h in range(4):
        @pl.when(z != h)
        def _():
            copy = direct(ctxs.at[h], ctxs.at[h], ("c2",), h, h, z=h)
            copy.wait_send()
            copy.wait_recv()

        copy = pltpu.make_async_copy(
            ctxs.at[h], ctx_out.at[:, pl.ds(h * HD, HD)], local_sem.at[local_ids("ctx", h)]
        )
        copy.start()
        copies_out.append(copy)

    out_finish(0)
    out_relay(1)
    out_finish(1)
    for t in range(4):
        itself = jnp.logical_and(z == t, jnp.logical_and(to_y == y, to_c == c))

        @pl.when(jnp.logical_not(itself))
        def _():
            for part in range(2):
                ref = cown.at[t, rows_of(part)]
                direct(ref, ref, ("cd", part), t, t, z=z).wait_send()

    for copy in sends:
        copy.wait_send()
    for copy in copies_out:
        copy.wait()


def on_device(hidden, norm_gain, w_query, w_key, w_value, w_out):
    block, width = hidden.shape
    wrows, cw = w_query.shape
    orows, ow = w_out.shape
    features = 8 * width
    tables = jnp.asarray(rotary_tables(block, 16))
    vmem = pl.BlockSpec(memory_space=pltpu.VMEM)

    def body(*refs):
        kernel(features, *refs)

    return pl.pallas_call(
        body,
        out_shape=(
            jax.ShapeDtypeStruct((block, cw), BF),
            jax.ShapeDtypeStruct((block, ow), BF),
        ),
        in_specs=[pl.BlockSpec(memory_space=pl.ANY)] * 5 + [vmem] * 2,
        out_specs=(pl.BlockSpec(memory_space=pl.ANY),) * 2,
        scratch_shapes=[
            pltpu.VMEM((12, block, width), BF),
            pltpu.VMEM((2, block // 2, width), BF),
            pltpu.VMEM((4, 2, 1, width), BF),
            pltpu.VMEM((2, 4, block, width), BF),
            pltpu.VMEM((4, block, HD), F32),
            pltpu.VMEM((4, 4, 8, block), F32),
            pltpu.VMEM((4 * block, HD), F32),
            pltpu.VMEM((3, 4, wrows, cw), BF),
            pltpu.VMEM((3, 4, 4 * block, HD), BF),
            pltpu.VMEM((3, 2, 2 * block, HD), BF),
            pltpu.VMEM((3, 2, 4 * block, HD), BF),
            pltpu.VMEM((2, 4, 4, block, HD), BF),
            pltpu.VMEM((4, block, HD), BF),
            pltpu.VMEM((4, block // 2, 4 * block), F32),
            pltpu.VMEM((10, block // 2, 4 * block), BF),
            pltpu.VMEM((4, block, HD), BF),
            pltpu.VMEM((2, 4, 4, block, HD), BF),
            pltpu.VMEM((4, block, HD), BF),
            pltpu.VMEM((4, orows, ow), BF),
            pltpu.VMEM((2 * block, 4 * orows), BF),
            pltpu.VMEM((4, block, ow), BF),
            pltpu.VMEM((2, 2, block // 4, ow), BF),
            pltpu.VMEM((2, block, ow), BF),
            pltpu.VMEM((block, ow), F32),
            pltpu.VMEM((block, ow), BF),
            pltpu.SemaphoreType.DMA((N_MESSAGES,)),
            pltpu.SemaphoreType.DMA((N_MESSAGES,)),
            pltpu.SemaphoreType.DMA((N_LOCAL,)),
        ],
        compiler_params=pltpu.CompilerParams(
            collective_id=0, has_side_effects=True, vmem_limit_bytes=62 * 1024 * 1024
        ),
    )(hidden, w_query, w_key, w_value, w_out, norm_gain.reshape(1, width), tables)


def solution(mesh):
    cube = Mesh(mesh.devices.reshape(4, 4, 4, 2), ("z", "y", "x", "c"))
    rows, cols = ("z", "y"), ("x", "c")
    both = P(rows, cols)
    return jax.shard_map(
        on_device,
        mesh=cube,
        in_specs=(both, P(cols), both, both, both, both),
        out_specs=(both, both),
        check_vma=False,
    )
```

```python
import math

import jax
import jax.numpy as jnp
import numpy as np
from jax import lax
from jax.experimental import pallas as pl
from jax.experimental.pallas import tpu as pltpu
from jax.sharding import Mesh, PartitionSpec as P

HD = 128
EPS = 1e-5
MESH = pl.DeviceIdType.MESH
BF = jnp.bfloat16
F32 = jnp.float32


def rotary_tables(block, blocks):
    freqs = np.exp(-math.log(10000.0) * 2.0 * np.arange(HD // 2) / HD)
    freqs = np.concatenate([freqs, freqs])[None, :]
    base = (np.arange(blocks) * block)[:, None] * freqs
    rows = np.arange(block)[:, None] * freqs
    angles = np.concatenate([base, rows], axis=0)
    return np.concatenate([np.cos(angles), np.sin(angles)], axis=1).astype(np.float32)


class Ids:
    def __init__(self):
        self.table = {}

    def __call__(self, *name):
        return self.table.setdefault(name, len(self.table))


N_MESSAGES = 132
N_LOCAL = 17
N_SENDS = 20


def kernel(
    features, hidden, wq, wk, wv, wout, gain, table_in,
    ctx_out, layer_out,
    big, transit, gbuf, tables, xs, ssq, sqs, rsc, wg, pbuf, tr, fin, kvg, qbuf, sbuf,
    probs, cown, cx, ctxs, wog, lhs, op, otr, ofin, oacc, lout, send_sem, recv_sem, local_sem,
):
    z, y, x, c = (lax.axis_index(n) for n in ("z", "y", "x", "c"))
    zr, zl, zf = (lax.rem(z + k, 4) for k in (1, 3, 2))
    yr, yl, yf = (lax.rem(y + k, 4) for k in (1, 3, 2))
    xr, xl, xf = (lax.rem(x + k, 4) for k in (1, 3, 2))
    other = 1 - c
    block = hidden.shape[0]
    half = block // 2
    ids, local_ids, small = Ids(), Ids(), Ids()
    unit = big.shape[1] * big.shape[2] // 8
    groups, classes = (2, 4, 8, 9), {}
    sends = []

    def group_of(src):
        size = math.prod(src.shape) * src.dtype.itemsize
        return size // unit if size % unit == 0 else 0

    def message(src, dst, name, **where):
        i = ids(*name)
        g = group_of(src)
        g = 9 if g == 8 and name[0][0] == "w" else g
        g = 0 if name[0] == "swap" else g
        classes[i] = g
        shared = groups.index(g) if g in groups else len(groups) + small(*name)
        return pltpu.make_async_remote_copy(
            src_ref=src, dst_ref=dst, send_sem=send_sem.at[shared], recv_sem=recv_sem.at[i],
            device_id=where, device_id_type=MESH,
        )

    def send(src, dst, name, **where):
        copy = message(src, dst, name, **where)
        copy.start()
        sends.append((name, copy))

    def drain():
        counts = {}
        for name, copy in sends:
            g = classes[ids(*name)]
            if g in groups:
                counts[g] = counts.get(g, 0) + 1
            else:
                copy.wait_send()
        for g, count in counts.items():
            lines_out = count * min(g, 8) * unit // (2 * big.shape[2])
            slots = max(n for n in range(1, 13) if lines_out % (16 * n) == 0 and lines_out // n <= big.shape[1])
            ref = big.at[pl.ds(0, slots), pl.ds(0, lines_out // slots)]
            pltpu.make_async_remote_copy(
                src_ref=ref, dst_ref=ref, send_sem=send_sem.at[groups.index(g)],
                recv_sem=recv_sem.at[0], device_id={"c": other}, device_id_type=MESH,
            ).wait_send()

    def arrived(dst, name, **where):
        message(dst, dst, name, **where).wait_recv()

    barrier = pltpu.get_barrier_semaphore()
    partners = [{"z": zr}, {"z": zl}, {"z": zf}, {"y": yr}, {"y": yl}, {"x": xr}, {"x": xl}, {"c": other}]
    for where in partners:
        pl.semaphore_signal(barrier, inc=1, device_id=where, device_id_type=MESH)

    def load(src, dst, name):
        copy = pltpu.make_async_copy(src, dst, local_sem.at[local_ids("load", name)])
        copy.start()
        return copy

    weights = {"k": wk, "v": wv, "q": wq}
    order = {"k": 0, "v": 1, "q": 2}
    score_factor = math.log2(math.e) / math.sqrt(HD)
    loads = {"x": load(hidden, big.at[x], "x")}
    for name in "kvq":
        loads[name] = load(weights[name], wg.at[order[name], y], name)
    loads["o"] = load(wout, wog.at[y], "o")
    loads["g"] = load(gain, gbuf.at[x, c], "g")
    loads["t"] = load(table_in, tables, "t")
    pl.semaphore_wait(barrier, len(partners))

    lines = {"y": (y, yr, yl, yf), "z": (z, zr, zl, zf)}

    def gather(axis, slot, name, pieces=(0, 1)):
        me, right, left, _ = lines[axis]
        for n in pieces:
            for h, side, to in ((n, "r", right), (1 - n, "l", left)):
                send(slot(me, h), slot(me, h), (name, side, h), **{axis: to})

    def forward(axis, slot, name):
        _, right, left, _ = lines[axis]
        arrived(slot(left, 0), (name, "r", 0), **{axis: right})
        send(slot(left, 0), slot(left, 0), (name, "fr"), **{axis: right})
        arrived(slot(right, 1), (name, "l", 1), **{axis: left})
        send(slot(right, 1), slot(right, 1), (name, "fl"), **{axis: left})

    def finish(axis, slot, name):
        _, right, left, far = lines[axis]
        arrived(slot(left, 1), (name, "r", 1), **{axis: right})
        arrived(slot(right, 0), (name, "l", 0), **{axis: left})
        arrived(slot(far, 0), (name, "fr"), **{axis: right})
        arrived(slot(far, 1), (name, "fl"), **{axis: left})

    def gather_y(slot, name):
        gather("y", slot, name)

    def forward_y(slot, name):
        forward("y", slot, name)

    def finish_y(slot, name):
        finish("y", slot, name)

    wrows = wk.shape[0]

    def weight_slot(name):
        def slot(owner, part):
            ref = wg.at[order[name], owner]
            return ref if part is None else ref.at[pl.ds(part * (wrows // 2), wrows // 2)]
        return slot

    class Spread:
        def __init__(self, name, buf, through):
            self.name, self.buf, self.through = name, buf, through
            self.rows = buf.shape[1] // 2

        def part(self, slot, h):
            return self.buf.at[slot, pl.ds(h * self.rows, self.rows)]

        def own(self, h):
            mine = self.part(x, h)
            send(mine, mine, (self.name, "xr", h), x=xr)
            send(mine, mine, (self.name, "xl", h), x=xl)
            self.onward(0, h)

        def pair(self, src_slot, owner, label, h):
            send(self.part(src_slot, h), self.part(8 + owner, h), (self.name, "pair", label, h), c=other)

        def onward(self, k, h):
            owner = lax.rem(x + k, 4)
            away = lax.rem(owner - z + 4, 4)
            src = self.part(owner, h)

            @pl.when(away == 0)
            def _():
                message(src, self.part(8 + z, h), (self.name, "pair", "own", h), c=other).start()

            @pl.when(away == 1)
            def _():
                message(src, self.part(4 + z, h), (self.name, "zr", h), z=zr).start()

            @pl.when(away == 3)
            def _():
                message(src, self.part(4 + z, h), (self.name, "zl", h), z=zl).start()

            @pl.when(away == 2)
            def _():
                to = {"z": zl} if h else {"z": zr}
                message(src, self.through.at[h], (self.name, "zz", h), **to).start()

            if k == 0:
                for label, where in (("zr", {"z": zr}), ("zl", {"z": zl}), ("zz", {"z": zl} if h else {"z": zr})):
                    name = (self.name, label, h)
                    sends.append((name, message(self.part(0, h), self.part(0, h), name, **where)))
                name = (self.name, "pair", "own", h)
                sends.append((name, message(self.part(0, h), self.part(0, h), name, c=other)))

        def from_left(self, h):
            mine = self.part(xl, h)
            arrived(mine, (self.name, "xr", h), x=xr)
            if h == 0:
                send(mine, mine, (self.name, "xf", 0), x=xr)
            self.onward(3, h)

        def from_right(self, h):
            mine = self.part(xr, h)
            arrived(mine, (self.name, "xl", h), x=xl)
            if h == 1:
                send(mine, mine, (self.name, "xf", 1), x=xl)
            self.onward(1, h)

        def from_far(self, h):
            where = {"x": xl} if h else {"x": xr}
            arrived(self.part(xf, h), (self.name, "xf", h), **where)
            self.onward(2, h)

        def pass_on(self, h):
            where = {"z": zl} if h else {"z": zr}
            arrived(self.through.at[h], (self.name, "zz", h), **where)
            send(self.through.at[h], self.part(4 + (zr if h else zl), h), (self.name, "zf", h), **where)

        def beside(self, which, h):
            owner, where = (zl, {"z": zr}) if which == "zr" else (zr, {"z": zl})
            arrived(self.part(4 + owner, h), (self.name, which, h), **where)
            self.pair(4 + owner, owner, which, h)

        def opposite(self, h):
            where = {"z": zl} if h else {"z": zr}
            arrived(self.part(4 + zf, h), (self.name, "zf", h), **where)
            self.pair(4 + zf, zf, "zf", h)

        def paired(self, owner, label):
            for h in range(2):
                arrived(self.part(8 + owner, h), (self.name, "pair", label, h), c=other)

    def process(slot, plane, t, first):
        g = gbuf[z, plane].astype(F32)
        width = big.shape[2]

        @pl.loop(0, block // 32)
        def _(i):
            r = pl.ds(pl.multiple_of(i * 32, 32), 32)
            total = None
            for k in range(width // HD):
                cols = slice(k * HD, (k + 1) * HD)
                v = big[slot, r, cols].astype(F32)
                xs[plane, t, r, cols] = (v * g[k:k + 1, :]).astype(BF)
                total = v * v if total is None else total + v * v
            if first:
                ssq[t, r, :] = total
            else:
                ssq[t, r, :] = ssq[t, r, :] + total

    spread = Spread("h", big, transit)
    loads["x"].wait()
    for h in range(2):
        spread.own(h)
    loads["k"].wait()
    gather_y(weight_slot("k"), "wk")
    loads["v"].wait()
    gather_y(weight_slot("v"), "wv")
    loads["g"].wait()
    gain_sends = [("r", {"x": xr}), ("l", {"x": xl}), ("c", {"c": other})]
    for label, where in gain_sends:
        send(gbuf.at[x, c], gbuf.at[x, c], ("gain", label), **where)
    spread.from_left(0)
    spread.from_right(0)
    spread.from_right(1)
    spread.from_left(1)
    arrived(gbuf.at[xl, c], ("gain", "r"), x=xr)
    send(gbuf.at[xl, c], gbuf.at[xl, c], ("gain", "rf"), x=xr)
    send(gbuf.at[xl, c], gbuf.at[xl, c], ("gain", "rc"), c=other)
    arrived(gbuf.at[xr, c], ("gain", "l"), x=xl)
    send(gbuf.at[xr, c], gbuf.at[xr, c], ("gain", "lc"), c=other)
    forward_y(weight_slot("k"), "wk")
    spread.from_far(0)
    spread.from_far(1)
    arrived(gbuf.at[xf, c], ("gain", "rf"), x=xr)
    send(gbuf.at[xf, c], gbuf.at[xf, c], ("gain", "fc"), c=other)
    spread.pass_on(0)
    spread.pass_on(1)
    arrived(gbuf.at[x, other], ("gain", "c"), c=other)
    arrived(gbuf.at[xl, other], ("gain", "rc"), c=other)
    arrived(gbuf.at[xr, other], ("gain", "lc"), c=other)
    arrived(gbuf.at[xf, other], ("gain", "fc"), c=other)
    process(z, c, z, True)
    forward_y(weight_slot("v"), "wv")
    loads["q"].wait()
    gather_y(weight_slot("q"), "wq")
    for which, owner in (("zr", zl), ("zl", zr)):
        for h in range(2):
            spread.beside(which, h)
        process(4 + owner, c, owner, True)
    spread.paired(z, "own")
    process(8 + z, other, z, False)
    for h in range(2):
        spread.opposite(h)
    process(4 + zf, c, zf, True)
    for label, owner in (("zr", zl), ("zl", zr), ("zf", zf)):
        spread.paired(owner, label)
        process(8 + owner, other, owner, False)
    for t in range(4):
        s = jnp.sum(ssq[t].T, axis=0, keepdims=True)
        sqs[z, t] = jnp.broadcast_to(s, (8, block))
    for where, label in ((zr, 1), (zl, 3), (zf, 2)):
        send(sqs.at[z], sqs.at[z], ("sq", label), z=where)

    cw = wk.shape[1]

    def lower(ref):
        return ref.at[pl.ds(0, 2 * block)]

    def upper(ref):
        return ref.at[pl.ds(2 * block, 2 * block)]

    def project(name):
        j = order[name]
        width = xs.shape[3]
        tokens = 4 * block

        @pl.loop(0, cw // 256)
        def _(n):
            cols = pl.ds(pl.multiple_of(n * 256, 256), 256)
            w0 = wg[j, 0:2, :, cols].reshape(width, 256)
            w1 = wg[j, 2:4, :, cols].reshape(width, 256)
            left0 = xs[0].reshape(tokens, width)
            left1 = xs[1].reshape(tokens, width)
            acc = jnp.dot(left0, w0, preferred_element_type=F32)
            acc = acc + jnp.dot(left1, w1, preferred_element_type=F32)
            pbuf[j, 2 * n] = acc[:, :HD].astype(BF)
            pbuf[j, 2 * n + 1] = acc[:, HD:].astype(BF)

    def scatter(name):
        j = order[name]
        send(lower(pbuf.at[j, zf]), tr.at[j, 0], (name, "ta"), z=zr)
        send(upper(pbuf.at[j, zf]), tr.at[j, 1], (name, "tb"), z=zl)
        send(upper(pbuf.at[j, zr]), upper(fin.at[j, 0]), (name, "a1"), z=zr)
        send(lower(pbuf.at[j, zl]), lower(fin.at[j, 1]), (name, "b0"), z=zl)

    def relay(name):
        j = order[name]
        lo, hi = pl.ds(0, 2 * block), pl.ds(2 * block, 2 * block)
        arrived(tr.at[j, 0], (name, "ta"), z=zr)
        pbuf[j, zr, lo, :] = (pbuf[j, zr, lo, :].astype(F32) + tr[j, 0].astype(F32)).astype(BF)
        send(lower(pbuf.at[j, zr]), lower(fin.at[j, 0]), (name, "a0"), z=zr)
        arrived(tr.at[j, 1], (name, "tb"), z=zl)
        pbuf[j, zl, hi, :] = (pbuf[j, zl, hi, :].astype(F32) + tr[j, 1].astype(F32)).astype(BF)
        send(upper(pbuf.at[j, zl]), upper(fin.at[j, 1]), (name, "b1"), z=zl)

    def reduced(name):
        j = order[name]
        arrived(upper(fin.at[j, 0]), (name, "a1"), z=zr)
        arrived(lower(fin.at[j, 1]), (name, "b0"), z=zl)
        arrived(lower(fin.at[j, 0]), (name, "a0"), z=zr)
        arrived(upper(fin.at[j, 1]), (name, "b1"), z=zl)

    def total_of(name, t):
        j = order[name]
        r = pl.ds(t * block, block)
        total = pbuf[j, z, r, :].astype(F32) + fin[j, 0, r, :].astype(F32) + fin[j, 1, r, :].astype(F32)
        return total * rsc[r, :]

    def rotated(v, t):
        bases = tables[:16, :]
        here = lax.broadcasted_iota(jnp.int32, bases.shape, 0) == 4 * t + y
        base = jnp.sum(jnp.where(here, bases, 0.0), axis=0, keepdims=True)
        ca, sa = base[:, :HD], base[:, HD:]
        ci, si = tables[16:, :HD], tables[16:, HD:]
        cos = ca * ci - sa * si
        sin = sa * ci + ca * si
        lane = lax.broadcasted_iota(jnp.int32, (block, HD), 1)
        signed = jnp.where(lane < HD // 2, -sin, sin)
        return v * cos + pltpu.roll(v, HD // 2, axis=1) * signed

    finish_y(weight_slot("k"), "wk")
    project("k")
    scatter("k")
    finish_y(weight_slot("v"), "wv")
    project("v")
    relay("k")
    scatter("v")

    for where, label in ((zr, 1), (zl, 3), (zf, 2)):
        src = {1: zl, 3: zr, 2: zf}[label]
        arrived(sqs.at[src], ("sq", label), z=where)
    for t in range(4):
        s = sqs[0, t] + sqs[1, t] + sqs[2, t] + sqs[3, t]
        factor = lax.rsqrt(s / features + EPS)
        rsc[pl.ds(t * block, block), :] = jnp.broadcast_to(factor[0:1, :], (HD, block)).T

    def kv_slot(which):
        def slot(owner, part):
            ref = kvg.at[which]
            return ref.at[:, owner] if part is None else ref.at[pl.ds(2 * part, 2), owner]
        return slot

    def out_slot(owner, part):
        ref = wog.at[owner]
        count = wout.shape[0] // 2
        return ref if part is None else ref.at[pl.ds(part * count, count)]

    forward_y(weight_slot("q"), "wq")
    loads["t"].wait()
    reduced("k")
    for t in range(4):
        kvg[0, t, y] = rotated(total_of("k", t), t).astype(BF)
    gather_y(kv_slot(0), "k")
    relay("v")
    finish_y(weight_slot("q"), "wq")
    project("q")
    scatter("q")
    forward_y(kv_slot(0), "k")
    reduced("v")
    for t in range(4):
        kvg[1, t, y] = total_of("v", t).astype(BF)
    gather_y(kv_slot(1), "v")
    relay("q")
    loads["o"].wait()
    forward_y(kv_slot(1), "v")
    gather("y", out_slot, "wo")
    reduced("q")
    for t in range(4):
        qbuf[t] = (rotated(total_of("q", t), t) * score_factor).astype(BF)
    finish_y(kv_slot(0), "k")

    span = 4 * block

    def keys(which, kb):
        return kvg[which, kb].reshape(span, HD)

    def base_of(name):
        return [ids(*name, k) for k in range(4)][0]

    def direct(src, dst, name, to, source, **where):
        first = base_of(name)
        small_base = [small(*name, k) for k in range(4)][0]
        return pltpu.make_async_remote_copy(
            src_ref=src, dst_ref=dst, send_sem=send_sem.at[len(groups) + small_base + to],
            recv_sem=recv_sem.at[first + source], device_id=where, device_id_type=MESH,
        )

    def rows_of(part):
        return pl.ds(part * half, half)

    def score_rows(part):
        mine = rows_of(part)
        for t in range(4):
            q = qbuf[t, mine, :]
            peak = None
            for kb in range(t + 1):
                s = lax.dot_general(q, keys(0, kb), (((1,), (1,)), ((), ())), preferred_element_type=F32)
                if kb == t:
                    row = lax.broadcasted_iota(jnp.int32, (half, span), 0) + (y * block + part * half)
                    col = lax.broadcasted_iota(jnp.int32, (half, span), 1)
                    s = jnp.where(col <= row, s, -jnp.inf)
                sbuf[t, kb] = s
                here = jnp.max(s, axis=1, keepdims=True)
                peak = here if peak is None else jnp.maximum(peak, here)
            for kb in range(t + 1):
                cols = slice(kb * span, (kb + 1) * span)
                probs[t, :, cols] = jnp.exp2(sbuf[t, kb] - peak).astype(BF)

    def context_rows(part):
        mine = rows_of(part)
        ones = jnp.ones((span, HD), BF)
        for t in range(4):
            acc = jnp.zeros((half, 2 * HD), F32)
            for kb in range(t + 1):
                right = jnp.concatenate([keys(1, kb), ones], axis=1)
                cols = slice(kb * span, (kb + 1) * span)
                acc = acc + jnp.dot(probs[t, :, cols], right, preferred_element_type=F32)
            cown[t, mine, :] = (acc[:, :HD] / acc[:, HD:]).astype(BF)
        swap(part, True)

    def swap(part, start):
        mine = rows_of(part)
        src, dst = cown.at[:, mine], cx.at[c, z, :, mine]
        copy = message(src, dst, ("swap", part), z=x, x=z)
        local = pltpu.make_async_copy(src, cx.at[c, x, :, mine], local_sem.at[local_ids("swap", part)])

        @pl.when(x != z)
        def _():
            if start:
                copy.start()
            else:
                copy.wait_recv()
                copy.wait_send()

        @pl.when(x == z)
        def _():
            if start:
                local.start()
            else:
                local.wait()

    def cx_part(plane, owner, part, h):
        return cx.at[plane, owner, pl.ds(2 * h, 2), rows_of(part)]

    def cx_pair(owner, label, part, h):
        mine = cx_part(c, owner, part, h)
        send(mine, mine, ("cp", label, part, h), c=other)

    def context_around(part):
        swap(part, False)
        for h, side, where in ((0, "cr", {"x": xr}), (1, "cl", {"x": xl}), (1, "cr", {"x": xr}), (0, "cl", {"x": xl})):
            send(cx_part(c, x, part, h), cx_part(c, x, part, h), (side, part, h), **where)
        for h in range(2):
            cx_pair(x, "own", part, h)

    def context_beside(part):
        left, right = cx_part(c, xl, part, 0), cx_part(c, xr, part, 1)
        arrived(left, ("cr", part, 0), x=xr)
        send(left, left, ("cf", part, 0), x=xr)
        cx_pair(xl, "left", part, 0)
        arrived(right, ("cl", part, 1), x=xl)
        send(right, right, ("cf", part, 1), x=xl)
        cx_pair(xr, "right", part, 1)

    def context_far(part):
        arrived(cx_part(c, xl, part, 1), ("cr", part, 1), x=xr)
        cx_pair(xl, "left", part, 1)
        arrived(cx_part(c, xr, part, 0), ("cl", part, 0), x=xl)
        cx_pair(xr, "right", part, 0)
        arrived(cx_part(c, xf, part, 0), ("cf", part, 0), x=xr)
        cx_pair(xf, "far", part, 0)
        arrived(cx_part(c, xf, part, 1), ("cf", part, 1), x=xl)
        cx_pair(xf, "far", part, 1)

    targets = (zf, zr, zl, z)

    def out_product(part):
        mine = rows_of(part)
        for label, owner in (("own", x), ("left", xl), ("right", xr), ("far", xf)):
            for h in range(2):
                arrived(cx_part(other, owner, part, h), ("cp", label, part, h), c=other)
        for i, d in enumerate(targets):
            for k in range(4):
                for p in range(2):
                    lhs[i * half:(i + 1) * half, (4 * p + k) * HD:(4 * p + k + 1) * HD] = cx[p, k, d, mine, :]
        depth = lhs.shape[1]

        @pl.loop(0, wog.shape[2] // 256)
        def _(n):
            cols = pl.ds(pl.multiple_of(n * 256, 256), 256)
            acc = jnp.dot(lhs[...], wog[:, :, cols].reshape(depth, 256), preferred_element_type=F32)
            for i in range(3):
                op[targets[i], mine, cols] = acc[i * half:(i + 1) * half].astype(BF)
            oacc[mine, cols] = acc[3 * half:]

    quarter = half // 2

    def piece(part, h):
        return pl.ds(part * half + h * quarter, quarter)

    def out_scatter(part):
        send(op.at[zf, piece(part, 0)], otr.at[part, 0], ("o", part, "ta"), z=zr)
        send(op.at[zf, piece(part, 1)], otr.at[part, 1], ("o", part, "tb"), z=zl)
        send(op.at[zr, piece(part, 1)], ofin.at[0, piece(part, 1)], ("o", part, "a1"), z=zr)
        send(op.at[zl, piece(part, 0)], ofin.at[1, piece(part, 0)], ("o", part, "b0"), z=zl)

    def out_relay(part):
        for h, to, where, came, name in ((0, zr, {"z": zr}, "ta", "a0"), (1, zl, {"z": zl}, "tb", "b1")):
            r = piece(part, h)
            arrived(otr.at[part, h], ("o", part, came), **where)
            op[to, r, :] = (op[to, r, :].astype(F32) + otr[part, h].astype(F32)).astype(BF)
            send(op.at[to, r], ofin.at[h, r], ("o", part, name), **where)

    copies_out = []

    def out_finish(part):
        arrived(ofin.at[0, piece(part, 1)], ("o", part, "a1"), z=zr)
        arrived(ofin.at[1, piece(part, 0)], ("o", part, "b0"), z=zl)
        for h, name, where in ((0, "a0", {"z": zr}), (1, "b1", {"z": zl})):
            r = piece(part, h)
            arrived(ofin.at[h, r], ("o", part, name), **where)
            total = big[x, r, :].astype(F32) + oacc[r, :]
            lout[r, :] = (total + ofin[0, r, :].astype(F32) + ofin[1, r, :].astype(F32)).astype(BF)
            copy = pltpu.make_async_copy(lout.at[r], layer_out.at[r], local_sem.at[local_ids("lout", part, h)])
            copy.start()
            copies_out.append(copy)

    score_rows(0)
    finish_y(kv_slot(1), "v")
    context_rows(0)
    score_rows(1)
    forward("y", out_slot, "wo")
    context_rows(1)
    context_around(0)
    for t in range(4):
        @pl.when(z != t)
        def _():
            direct(cown.at[t], ctxs.at[z], ("c2",), t, z, z=t).start()

        @pl.when(z == t)
        def _():
            ctxs[z] = cown[t]

    context_beside(0)
    context_around(1)
    context_far(0)
    context_beside(1)
    finish("y", out_slot, "wo")
    out_product(0)
    out_scatter(0)
    context_far(1)
    out_relay(0)
    out_product(1)
    out_scatter(1)

    for h in range(4):
        @pl.when(z != h)
        def _():
            copy = direct(ctxs.at[h], ctxs.at[h], ("c2",), h, h, z=h)
            copy.wait_send()
            copy.wait_recv()

        copy = pltpu.make_async_copy(
            ctxs.at[h], ctx_out.at[:, pl.ds(h * HD, HD)], local_sem.at[local_ids("ctx", h)]
        )
        copy.start()
        copies_out.append(copy)

    out_finish(0)
    out_relay(1)
    out_finish(1)
    drain()
    for copy in copies_out:
        copy.wait()


def on_device(hidden, norm_gain, w_query, w_key, w_value, w_out):
    block, width = hidden.shape
    wrows, cw = w_query.shape
    orows, ow = w_out.shape
    features = 8 * width
    tables = jnp.asarray(rotary_tables(block, 16))

    def body(*refs):
        kernel(features, *refs)

    return pl.pallas_call(
        body,
        out_shape=(
            jax.ShapeDtypeStruct((block, cw), BF),
            jax.ShapeDtypeStruct((block, ow), BF),
        ),
        in_specs=[pl.BlockSpec(memory_space=pl.ANY)] * 7,
        out_specs=(pl.BlockSpec(memory_space=pl.ANY),) * 2,
        scratch_shapes=[
            pltpu.VMEM((12, block, width), BF),
            pltpu.VMEM((2, block // 2, width), BF),
            pltpu.VMEM((4, 2, width // HD, HD), BF),
            pltpu.VMEM((16 + block, 2 * HD), F32),
            pltpu.VMEM((2, 4, block, width), BF),
            pltpu.VMEM((4, block, HD), F32),
            pltpu.VMEM((4, 4, 8, block), F32),
            pltpu.VMEM((4 * block, HD), F32),
            pltpu.VMEM((3, 4, wrows, cw), BF),
            pltpu.VMEM((3, 4, 4 * block, HD), BF),
            pltpu.VMEM((3, 2, 2 * block, HD), BF),
            pltpu.VMEM((3, 2, 4 * block, HD), BF),
            pltpu.VMEM((2, 4, 4, block, HD), BF),
            pltpu.VMEM((4, block, HD), BF),
            pltpu.VMEM((4, 4, block // 2, 4 * block), F32),
            pltpu.VMEM((4, block // 2, 16 * block), BF),
            pltpu.VMEM((4, block, HD), BF),
            pltpu.VMEM((2, 4, 4, block, HD), BF),
            pltpu.VMEM((4, block, HD), BF),
            pltpu.VMEM((4, orows, ow), BF),
            pltpu.VMEM((2 * block, 4 * orows), BF),
            pltpu.VMEM((4, block, ow), BF),
            pltpu.VMEM((2, 2, block // 4, ow), BF),
            pltpu.VMEM((2, block, ow), BF),
            pltpu.VMEM((block, ow), F32),
            pltpu.VMEM((block, ow), BF),
            pltpu.SemaphoreType.DMA((N_SENDS,)),
            pltpu.SemaphoreType.DMA((N_MESSAGES,)),
            pltpu.SemaphoreType.DMA((N_LOCAL,)),
        ],
        compiler_params=pltpu.CompilerParams(
            collective_id=0, has_side_effects=True, vmem_limit_bytes=62 * 1024 * 1024
        ),
    )(hidden, w_query, w_key, w_value, w_out, norm_gain.reshape(width // HD, HD), tables)


def solution(mesh):
    cube = Mesh(mesh.devices.reshape(4, 4, 4, 2), ("z", "y", "x", "c"))
    rows, cols = ("z", "y"), ("x", "c")
    both = P(rows, cols)
    return jax.shard_map(
        on_device,
        mesh=cube,
        in_specs=(both, P(cols), both, both, both, both),
        out_specs=(both, both),
        check_vma=False,
    )
```

```python
import math

import jax
import jax.numpy as jnp
import numpy as np
from jax import lax
from jax.experimental import pallas as pl
from jax.experimental.pallas import tpu as pltpu
from jax.sharding import Mesh, PartitionSpec as P

HD = 128
EPS = 1e-5
MESH = pl.DeviceIdType.MESH
BF = jnp.bfloat16
F32 = jnp.float32


def rotary_tables(block, blocks):
    freqs = np.exp(-math.log(10000.0) * 2.0 * np.arange(HD // 2) / HD)
    freqs = np.concatenate([freqs, freqs])[None, :]
    base = (np.arange(blocks) * block)[:, None] * freqs
    rows = np.arange(block)[:, None] * freqs
    angles = np.concatenate([base, rows], axis=0)
    return np.concatenate([np.cos(angles), np.sin(angles)], axis=1).astype(np.float32)


class Ids:
    def __init__(self):
        self.table = {}

    def __call__(self, *name):
        return self.table.setdefault(name, len(self.table))


N_MESSAGES = 132
N_LOCAL = 9
N_SENDS = 20


def kernel(
    features, hidden, wq, wk, wv, wout, gain, table_in,
    ctx_out, layer_out,
    big, transit, gbuf, tables, xs, ssq, sqs, rsc, wg, pbuf, tr, fin, kvg, qbuf, sbuf,
    probs, cown, cx, ctxs, wog, lhs, op, otr, ofin, oacc, send_sem, recv_sem, local_sem,
):
    z, y, x, c = (lax.axis_index(n) for n in ("z", "y", "x", "c"))
    zr, zl, zf = (lax.rem(z + k, 4) for k in (1, 3, 2))
    yr, yl, yf = (lax.rem(y + k, 4) for k in (1, 3, 2))
    xr, xl, xf = (lax.rem(x + k, 4) for k in (1, 3, 2))
    other = 1 - c
    block = hidden.shape[0]
    half = block // 2
    ids, local_ids, small = Ids(), Ids(), Ids()
    unit = big.shape[1] * big.shape[2] // 8
    groups, classes = (2, 4, 8, 9), {}
    sends = []

    def group_of(src):
        size = math.prod(src.shape) * src.dtype.itemsize
        return size // unit if size % unit == 0 else 0

    def message(src, dst, name, **where):
        i = ids(*name)
        g = group_of(src)
        g = 9 if g == 8 and name[0][0] == "w" else g
        g = 0 if name[0] == "swap" else g
        classes[i] = g
        shared = groups.index(g) if g in groups else len(groups) + small(*name)
        return pltpu.make_async_remote_copy(
            src_ref=src, dst_ref=dst, send_sem=send_sem.at[shared], recv_sem=recv_sem.at[i],
            device_id=where, device_id_type=MESH,
        )

    def send(src, dst, name, **where):
        copy = message(src, dst, name, **where)
        copy.start()
        sends.append((name, copy))

    def drain():
        counts = {}
        for name, copy in sends:
            g = classes[ids(*name)]
            if g in groups:
                counts[g] = counts.get(g, 0) + 1
            else:
                copy.wait_send()
        for g, count in counts.items():
            lines_out = count * min(g, 8) * unit // (2 * big.shape[2])
            slots = max(n for n in range(1, 13) if lines_out % (16 * n) == 0 and lines_out // n <= big.shape[1])
            ref = big.at[pl.ds(0, slots), pl.ds(0, lines_out // slots)]
            pltpu.make_async_remote_copy(
                src_ref=ref, dst_ref=ref, send_sem=send_sem.at[groups.index(g)],
                recv_sem=recv_sem.at[0], device_id={"c": other}, device_id_type=MESH,
            ).wait_send()

    def arrived(dst, name, **where):
        message(dst, dst, name, **where).wait_recv()

    barrier = pltpu.get_barrier_semaphore()
    partners = [{"z": zr}, {"z": zl}, {"z": zf}, {"y": yr}, {"y": yl}, {"x": xr}, {"x": xl}, {"c": other}]
    for where in partners:
        pl.semaphore_signal(barrier, inc=1, device_id=where, device_id_type=MESH)

    def load(src, dst, name):
        copy = pltpu.make_async_copy(src, dst, local_sem.at[local_ids("load", name)])
        copy.start()
        return copy

    weights = {"k": wk, "v": wv, "q": wq}
    order = {"k": 0, "v": 1, "q": 2}
    score_factor = math.log2(math.e) / math.sqrt(HD)
    loads = {"x": load(hidden, big.at[x], "x")}
    for name in "kvq":
        loads[name] = load(weights[name], wg.at[order[name], y], name)
    loads["o"] = load(wout, wog.at[y], "o")
    loads["g"] = load(gain, gbuf.at[x, c], "g")
    loads["t"] = load(table_in, tables, "t")
    pl.semaphore_wait(barrier, len(partners))

    lines = {"y": (y, yr, yl, yf), "z": (z, zr, zl, zf)}

    def gather(axis, slot, name, pieces=(0, 1)):
        me, right, left, _ = lines[axis]
        for n in pieces:
            for h, side, to in ((n, "r", right), (1 - n, "l", left)):
                send(slot(me, h), slot(me, h), (name, side, h), **{axis: to})

    def forward(axis, slot, name):
        _, right, left, _ = lines[axis]
        arrived(slot(left, 0), (name, "r", 0), **{axis: right})
        send(slot(left, 0), slot(left, 0), (name, "fr"), **{axis: right})
        arrived(slot(right, 1), (name, "l", 1), **{axis: left})
        send(slot(right, 1), slot(right, 1), (name, "fl"), **{axis: left})

    def finish(axis, slot, name):
        _, right, left, far = lines[axis]
        arrived(slot(left, 1), (name, "r", 1), **{axis: right})
        arrived(slot(right, 0), (name, "l", 0), **{axis: left})
        arrived(slot(far, 0), (name, "fr"), **{axis: right})
        arrived(slot(far, 1), (name, "fl"), **{axis: left})

    def gather_y(slot, name):
        gather("y", slot, name)

    def forward_y(slot, name):
        forward("y", slot, name)

    def finish_y(slot, name):
        finish("y", slot, name)

    wrows = wk.shape[0]

    def weight_slot(name):
        def slot(owner, part):
            ref = wg.at[order[name], owner]
            return ref if part is None else ref.at[pl.ds(part * (wrows // 2), wrows // 2)]
        return slot

    class Spread:
        def __init__(self, name, buf, through):
            self.name, self.buf, self.through = name, buf, through
            self.rows = buf.shape[1] // 2

        def part(self, slot, h):
            return self.buf.at[slot, pl.ds(h * self.rows, self.rows)]

        def own(self):
            for h, side, to in ((0, "xr", xr), (1, "xl", xl), (1, "xr", xr), (0, "xl", xl)):
                mine = self.part(x, h)
                send(mine, mine, (self.name, side, h), x=to)
            self.onward(0, 0)
            self.onward(0, 1)

        def pair(self, src_slot, owner, label, h):
            send(self.part(src_slot, h), self.part(8 + owner, h), (self.name, "pair", label, h), c=other)

        def onward(self, k, h):
            owner = lax.rem(x + k, 4)
            away = lax.rem(owner - z + 4, 4)
            src = self.part(owner, h)

            @pl.when(away == 0)
            def _():
                message(src, self.part(8 + z, h), (self.name, "pair", "own", h), c=other).start()

            @pl.when(away == 1)
            def _():
                message(src, self.part(4 + z, h), (self.name, "zr", h), z=zr).start()

            @pl.when(away == 3)
            def _():
                message(src, self.part(4 + z, h), (self.name, "zl", h), z=zl).start()

            @pl.when(away == 2)
            def _():
                to = {"z": zl} if h else {"z": zr}
                message(src, self.through.at[h], (self.name, "zz", h), **to).start()

            if k == 0:
                for label, where in (("zr", {"z": zr}), ("zl", {"z": zl}), ("zz", {"z": zl} if h else {"z": zr})):
                    name = (self.name, label, h)
                    sends.append((name, message(self.part(0, h), self.part(0, h), name, **where)))
                name = (self.name, "pair", "own", h)
                sends.append((name, message(self.part(0, h), self.part(0, h), name, c=other)))

        def from_left(self, h):
            mine = self.part(xl, h)
            arrived(mine, (self.name, "xr", h), x=xr)
            if h == 0:
                send(mine, mine, (self.name, "xf", 0), x=xr)
            self.onward(3, h)

        def from_right(self, h):
            mine = self.part(xr, h)
            arrived(mine, (self.name, "xl", h), x=xl)
            if h == 1:
                send(mine, mine, (self.name, "xf", 1), x=xl)
            self.onward(1, h)

        def from_far(self, h):
            where = {"x": xl} if h else {"x": xr}
            arrived(self.part(xf, h), (self.name, "xf", h), **where)
            self.onward(2, h)

        def pass_on(self, h):
            where = {"z": zl} if h else {"z": zr}
            arrived(self.through.at[h], (self.name, "zz", h), **where)
            send(self.through.at[h], self.part(4 + (zr if h else zl), h), (self.name, "zf", h), **where)

        def beside(self, which, h):
            owner, where = (zl, {"z": zr}) if which == "zr" else (zr, {"z": zl})
            arrived(self.part(4 + owner, h), (self.name, which, h), **where)
            self.pair(4 + owner, owner, which, h)

        def opposite(self, h):
            where = {"z": zl} if h else {"z": zr}
            arrived(self.part(4 + zf, h), (self.name, "zf", h), **where)
            self.pair(4 + zf, zf, "zf", h)

        def paired(self, owner, label):
            for h in range(2):
                arrived(self.part(8 + owner, h), (self.name, "pair", label, h), c=other)

    def process(slot, plane, t, first):
        g = gbuf[z, plane].astype(F32)
        width = big.shape[2]

        @pl.loop(0, block // 32)
        def _(i):
            r = pl.ds(pl.multiple_of(i * 32, 32), 32)
            total = None
            for k in range(width // HD):
                cols = slice(k * HD, (k + 1) * HD)
                v = big[slot, r, cols].astype(F32)
                xs[plane, t, r, cols] = (v * g[k:k + 1, :]).astype(BF)
                total = v * v if total is None else total + v * v
            if first:
                ssq[t, r, :] = total
            else:
                ssq[t, r, :] = ssq[t, r, :] + total

    spread = Spread("h", big, transit)
    loads["x"].wait()
    spread.own()
    loads["k"].wait()
    gather_y(weight_slot("k"), "wk")
    loads["v"].wait()
    gather_y(weight_slot("v"), "wv")
    loads["g"].wait()
    gain_sends = [("r", {"x": xr}), ("l", {"x": xl}), ("c", {"c": other})]
    for label, where in gain_sends:
        send(gbuf.at[x, c], gbuf.at[x, c], ("gain", label), **where)
    spread.from_left(0)
    spread.from_right(1)
    spread.from_right(0)
    spread.from_left(1)
    arrived(gbuf.at[xl, c], ("gain", "r"), x=xr)
    send(gbuf.at[xl, c], gbuf.at[xl, c], ("gain", "rf"), x=xr)
    send(gbuf.at[xl, c], gbuf.at[xl, c], ("gain", "rc"), c=other)
    arrived(gbuf.at[xr, c], ("gain", "l"), x=xl)
    send(gbuf.at[xr, c], gbuf.at[xr, c], ("gain", "lc"), c=other)
    forward_y(weight_slot("k"), "wk")
    spread.from_far(0)
    spread.from_far(1)
    arrived(gbuf.at[xf, c], ("gain", "rf"), x=xr)
    send(gbuf.at[xf, c], gbuf.at[xf, c], ("gain", "fc"), c=other)
    spread.pass_on(0)
    spread.pass_on(1)
    arrived(gbuf.at[x, other], ("gain", "c"), c=other)
    arrived(gbuf.at[xl, other], ("gain", "rc"), c=other)
    arrived(gbuf.at[xr, other], ("gain", "lc"), c=other)
    arrived(gbuf.at[xf, other], ("gain", "fc"), c=other)
    process(z, c, z, True)
    forward_y(weight_slot("v"), "wv")
    loads["q"].wait()
    gather_y(weight_slot("q"), "wq")
    for which, owner in (("zr", zl), ("zl", zr)):
        for h in range(2):
            spread.beside(which, h)
        process(4 + owner, c, owner, True)
    spread.paired(z, "own")
    process(8 + z, other, z, False)
    for h in range(2):
        spread.opposite(h)
    process(4 + zf, c, zf, True)
    for label, owner in (("zr", zl), ("zl", zr), ("zf", zf)):
        spread.paired(owner, label)
        process(8 + owner, other, owner, False)
    for t in range(4):
        s = jnp.sum(ssq[t].T, axis=0, keepdims=True)
        sqs[z, t] = jnp.broadcast_to(s, (8, block))
    for where, label in ((zr, 1), (zl, 3), (zf, 2)):
        send(sqs.at[z], sqs.at[z], ("sq", label), z=where)

    cw = wk.shape[1]

    def lower(ref):
        return ref.at[pl.ds(0, 2 * block)]

    def upper(ref):
        return ref.at[pl.ds(2 * block, 2 * block)]

    def project(name):
        j = order[name]
        width = xs.shape[3]
        tokens = 4 * block

        @pl.loop(0, cw // 256)
        def _(n):
            cols = pl.ds(pl.multiple_of(n * 256, 256), 256)
            w0 = wg[j, 0:2, :, cols].reshape(width, 256)
            w1 = wg[j, 2:4, :, cols].reshape(width, 256)
            left0 = xs[0].reshape(tokens, width)
            left1 = xs[1].reshape(tokens, width)
            acc = jnp.dot(left0, w0, preferred_element_type=F32)
            acc = acc + jnp.dot(left1, w1, preferred_element_type=F32)
            pbuf[j, 2 * n] = acc[:, :HD].astype(BF)
            pbuf[j, 2 * n + 1] = acc[:, HD:].astype(BF)

    def scatter(name):
        j = order[name]
        send(lower(pbuf.at[j, zf]), tr.at[j, 0], (name, "ta"), z=zr)
        send(upper(pbuf.at[j, zf]), tr.at[j, 1], (name, "tb"), z=zl)
        send(upper(pbuf.at[j, zr]), upper(fin.at[j, 0]), (name, "a1"), z=zr)
        send(lower(pbuf.at[j, zl]), lower(fin.at[j, 1]), (name, "b0"), z=zl)

    def relay(name):
        j = order[name]
        lo, hi = pl.ds(0, 2 * block), pl.ds(2 * block, 2 * block)
        arrived(tr.at[j, 0], (name, "ta"), z=zr)
        pbuf[j, zr, lo, :] = (pbuf[j, zr, lo, :].astype(F32) + tr[j, 0].astype(F32)).astype(BF)
        send(lower(pbuf.at[j, zr]), lower(fin.at[j, 0]), (name, "a0"), z=zr)
        arrived(tr.at[j, 1], (name, "tb"), z=zl)
        pbuf[j, zl, hi, :] = (pbuf[j, zl, hi, :].astype(F32) + tr[j, 1].astype(F32)).astype(BF)
        send(upper(pbuf.at[j, zl]), upper(fin.at[j, 1]), (name, "b1"), z=zl)

    def reduced(name):
        j = order[name]
        arrived(upper(fin.at[j, 0]), (name, "a1"), z=zr)
        arrived(lower(fin.at[j, 1]), (name, "b0"), z=zl)
        arrived(lower(fin.at[j, 0]), (name, "a0"), z=zr)
        arrived(upper(fin.at[j, 1]), (name, "b1"), z=zl)

    def total_of(name, t):
        j = order[name]
        r = pl.ds(t * block, block)
        total = pbuf[j, z, r, :].astype(F32) + fin[j, 0, r, :].astype(F32) + fin[j, 1, r, :].astype(F32)
        return total * rsc[r, :]

    def rotated(v, t):
        bases = tables[:16, :]
        here = lax.broadcasted_iota(jnp.int32, bases.shape, 0) == 4 * t + y
        base = jnp.sum(jnp.where(here, bases, 0.0), axis=0, keepdims=True)
        ca, sa = base[:, :HD], base[:, HD:]
        ci, si = tables[16:, :HD], tables[16:, HD:]
        cos = ca * ci - sa * si
        sin = sa * ci + ca * si
        lane = lax.broadcasted_iota(jnp.int32, (block, HD), 1)
        signed = jnp.where(lane < HD // 2, -sin, sin)
        return v * cos + pltpu.roll(v, HD // 2, axis=1) * signed

    finish_y(weight_slot("k"), "wk")
    project("k")
    scatter("k")
    finish_y(weight_slot("v"), "wv")
    project("v")
    relay("k")
    scatter("v")

    for where, label in ((zr, 1), (zl, 3), (zf, 2)):
        src = {1: zl, 3: zr, 2: zf}[label]
        arrived(sqs.at[src], ("sq", label), z=where)
    for t in range(4):
        s = sqs[0, t] + sqs[1, t] + sqs[2, t] + sqs[3, t]
        factor = lax.rsqrt(s / features + EPS)
        rsc[pl.ds(t * block, block), :] = jnp.broadcast_to(factor[0:1, :], (HD, block)).T

    def kv_slot(which):
        def slot(owner, part):
            ref = kvg.at[which]
            return ref.at[:, owner] if part is None else ref.at[pl.ds(2 * part, 2), owner]
        return slot

    def out_slot(owner, part):
        ref = wog.at[owner]
        count = wout.shape[0] // 2
        return ref if part is None else ref.at[pl.ds(part * count, count)]

    forward_y(weight_slot("q"), "wq")
    loads["t"].wait()
    reduced("k")
    for t in range(4):
        kvg[0, t, y] = rotated(total_of("k", t), t).astype(BF)
    gather_y(kv_slot(0), "k")
    relay("v")
    finish_y(weight_slot("q"), "wq")
    project("q")
    scatter("q")
    forward_y(kv_slot(0), "k")
    reduced("v")
    for t in range(4):
        kvg[1, t, y] = total_of("v", t).astype(BF)
    gather_y(kv_slot(1), "v")
    relay("q")
    loads["o"].wait()
    forward_y(kv_slot(1), "v")
    gather("y", out_slot, "wo")
    reduced("q")
    for t in range(4):
        qbuf[t] = (rotated(total_of("q", t), t) * score_factor).astype(BF)
    finish_y(kv_slot(0), "k")

    span = 4 * block

    def keys(which, kb):
        return kvg[which, kb].reshape(span, HD)

    def base_of(name):
        return [ids(*name, k) for k in range(4)][0]

    def direct(src, dst, name, to, source, **where):
        first = base_of(name)
        small_base = [small(*name, k) for k in range(4)][0]
        return pltpu.make_async_remote_copy(
            src_ref=src, dst_ref=dst, send_sem=send_sem.at[len(groups) + small_base + to],
            recv_sem=recv_sem.at[first + source], device_id=where, device_id_type=MESH,
        )

    def rows_of(part):
        return pl.ds(part * half, half)

    def score_rows(part):
        mine = rows_of(part)
        for t in range(4):
            q = qbuf[t, mine, :]
            peak = None
            for kb in range(t + 1):
                s = lax.dot_general(q, keys(0, kb), (((1,), (1,)), ((), ())), preferred_element_type=F32)
                if kb == t:
                    row = lax.broadcasted_iota(jnp.int32, (half, span), 0) + (y * block + part * half)
                    col = lax.broadcasted_iota(jnp.int32, (half, span), 1)
                    s = jnp.where(col <= row, s, -jnp.inf)
                sbuf[t, kb] = s
                here = jnp.max(s, axis=1, keepdims=True)
                peak = here if peak is None else jnp.maximum(peak, here)
            for kb in range(t + 1):
                cols = slice(kb * span, (kb + 1) * span)
                probs[t, :, cols] = jnp.exp2(sbuf[t, kb] - peak).astype(BF)

    def context_rows(part):
        mine = rows_of(part)
        ones = jnp.ones((span, HD), BF)
        for t in range(4):
            acc = jnp.zeros((half, 2 * HD), F32)
            for kb in range(t + 1):
                right = jnp.concatenate([keys(1, kb), ones], axis=1)
                cols = slice(kb * span, (kb + 1) * span)
                acc = acc + jnp.dot(probs[t, :, cols], right, preferred_element_type=F32)
            cown[t, mine, :] = (acc[:, :HD] / acc[:, HD:]).astype(BF)
        swap(part, True)

    def swap(part, start):
        mine = rows_of(part)
        src, dst = cown.at[:, mine], cx.at[c, z, :, mine]
        copy = message(src, dst, ("swap", part), z=x, x=z)
        local = pltpu.make_async_copy(src, cx.at[c, x, :, mine], local_sem.at[local_ids("swap", part)])

        @pl.when(x != z)
        def _():
            if start:
                copy.start()
            else:
                copy.wait_recv()
                copy.wait_send()

        @pl.when(x == z)
        def _():
            if start:
                local.start()
            else:
                local.wait()

    def cx_part(plane, owner, part, h):
        return cx.at[plane, owner, pl.ds(2 * h, 2), rows_of(part)]

    def cx_pair(owner, label, part, h):
        mine = cx_part(c, owner, part, h)
        send(mine, mine, ("cp", label, part, h), c=other)

    def context_around(part):
        swap(part, False)
        for h, side, where in ((0, "cr", {"x": xr}), (1, "cl", {"x": xl}), (1, "cr", {"x": xr}), (0, "cl", {"x": xl})):
            send(cx_part(c, x, part, h), cx_part(c, x, part, h), (side, part, h), **where)
        for h in range(2):
            cx_pair(x, "own", part, h)

    def context_beside(part):
        left, right = cx_part(c, xl, part, 0), cx_part(c, xr, part, 1)
        arrived(left, ("cr", part, 0), x=xr)
        send(left, left, ("cf", part, 0), x=xr)
        cx_pair(xl, "left", part, 0)
        arrived(right, ("cl", part, 1), x=xl)
        send(right, right, ("cf", part, 1), x=xl)
        cx_pair(xr, "right", part, 1)

    def context_far(part):
        arrived(cx_part(c, xl, part, 1), ("cr", part, 1), x=xr)
        cx_pair(xl, "left", part, 1)
        arrived(cx_part(c, xr, part, 0), ("cl", part, 0), x=xl)
        cx_pair(xr, "right", part, 0)
        arrived(cx_part(c, xf, part, 0), ("cf", part, 0), x=xr)
        cx_pair(xf, "far", part, 0)
        arrived(cx_part(c, xf, part, 1), ("cf", part, 1), x=xl)
        cx_pair(xf, "far", part, 1)

    targets = (zf, zr, zl, z)

    def out_product(part):
        mine = rows_of(part)
        for label, owner in (("own", x), ("left", xl), ("right", xr), ("far", xf)):
            for h in range(2):
                arrived(cx_part(other, owner, part, h), ("cp", label, part, h), c=other)
        depth = lhs.shape[1]

        def product(first_target, count):
            for i in range(first_target, first_target + count):
                for k in range(4):
                    for p in range(2):
                        lhs[i * half:(i + 1) * half, (4 * p + k) * HD:(4 * p + k + 1) * HD] = cx[p, k, targets[i], mine, :]

            @pl.loop(0, wog.shape[2] // 256)
            def _(n):
                cols = pl.ds(pl.multiple_of(n * 256, 256), 256)
                left = lhs[first_target * half:(first_target + count) * half, :]
                acc = jnp.dot(left, wog[:, :, cols].reshape(depth, 256), preferred_element_type=F32)
                for i in range(first_target, first_target + count):
                    rows = slice((i - first_target) * half, (i - first_target + 1) * half)
                    if i < 3:
                        op[targets[i], mine, cols] = acc[rows].astype(BF)
                    else:
                        oacc[mine, cols] = acc[rows]

        if part == 0:
            product(0, 1)
            out_across(part)
            product(1, 3)
            out_scatter(part)
        else:
            product(0, 4)

    quarter = half // 2

    def piece(part, h):
        return pl.ds(part * half + h * quarter, quarter)

    def out_across(part):
        send(op.at[zf, piece(part, 0)], otr.at[part, 0], ("o", part, "ta"), z=zr)
        send(op.at[zf, piece(part, 1)], otr.at[part, 1], ("o", part, "tb"), z=zl)

    def out_scatter(part):
        send(op.at[zr, piece(part, 1)], ofin.at[0, piece(part, 1)], ("o", part, "a1"), z=zr)
        send(op.at[zl, piece(part, 0)], ofin.at[1, piece(part, 0)], ("o", part, "b0"), z=zl)

    def out_relay(part):
        for h, to, where, came, name in ((0, zr, {"z": zr}, "ta", "a0"), (1, zl, {"z": zl}, "tb", "b1")):
            r = piece(part, h)
            arrived(otr.at[part, h], ("o", part, came), **where)
            op[to, r, :] = (op[to, r, :].astype(F32) + otr[part, h].astype(F32)).astype(BF)
            send(op.at[to, r], ofin.at[h, r], ("o", part, name), **where)

    def out_finish(part):
        arrived(ofin.at[0, piece(part, 1)], ("o", part, "a1"), z=zr)
        arrived(ofin.at[1, piece(part, 0)], ("o", part, "b0"), z=zl)
        for h, name, where in ((0, "a0", {"z": zr}), (1, "b1", {"z": zl})):
            r = piece(part, h)
            arrived(ofin.at[h, r], ("o", part, name), **where)
            total = big[x, r, :].astype(F32) + oacc[r, :]
            layer_out[r, :] = (total + ofin[0, r, :].astype(F32) + ofin[1, r, :].astype(F32)).astype(BF)

    score_rows(0)
    finish_y(kv_slot(1), "v")
    context_rows(0)
    score_rows(1)
    forward("y", out_slot, "wo")
    context_rows(1)
    context_around(0)
    for t in range(4):
        @pl.when(z != t)
        def _():
            direct(cown.at[t], ctxs.at[z], ("c2",), t, z, z=t).start()

        @pl.when(z == t)
        def _():
            ctxs[z] = cown[t]

    context_beside(0)
    context_around(1)
    context_far(0)
    finish("y", out_slot, "wo")
    out_product(0)
    context_beside(1)
    context_far(1)
    out_relay(0)
    out_product(1)
    out_across(1)
    out_scatter(1)

    for h in range(4):
        @pl.when(z != h)
        def _():
            copy = direct(ctxs.at[h], ctxs.at[h], ("c2",), h, h, z=h)
            copy.wait_send()
            copy.wait_recv()

        ctx_out[:, h * HD:(h + 1) * HD] = ctxs[h]

    out_finish(0)
    out_relay(1)
    out_finish(1)
    drain()


def on_device(hidden, norm_gain, w_query, w_key, w_value, w_out):
    block, width = hidden.shape
    wrows, cw = w_query.shape
    orows, ow = w_out.shape
    features = 8 * width
    tables = jnp.asarray(rotary_tables(block, 16))

    def body(*refs):
        kernel(features, *refs)

    return pl.pallas_call(
        body,
        out_shape=(
            pltpu.VMEM((block, cw), BF),
            pltpu.VMEM((block, ow), BF),
        ),
        in_specs=[pl.BlockSpec(memory_space=pl.ANY)] * 7,
        out_specs=(pl.BlockSpec(memory_space=pltpu.VMEM),) * 2,
        scratch_shapes=[
            pltpu.VMEM((12, block, width), BF),
            pltpu.VMEM((2, block // 2, width), BF),
            pltpu.VMEM((4, 2, width // HD, HD), BF),
            pltpu.VMEM((16 + block, 2 * HD), F32),
            pltpu.VMEM((2, 4, block, width), BF),
            pltpu.VMEM((4, block, HD), F32),
            pltpu.VMEM((4, 4, 8, block), F32),
            pltpu.VMEM((4 * block, HD), F32),
            pltpu.VMEM((3, 4, wrows, cw), BF),
            pltpu.VMEM((3, 4, 4 * block, HD), BF),
            pltpu.VMEM((3, 2, 2 * block, HD), BF),
            pltpu.VMEM((3, 2, 4 * block, HD), BF),
            pltpu.VMEM((2, 4, 4, block, HD), BF),
            pltpu.VMEM((4, block, HD), BF),
            pltpu.VMEM((4, 4, block // 2, 4 * block), F32),
            pltpu.VMEM((4, block // 2, 16 * block), BF),
            pltpu.VMEM((4, block, HD), BF),
            pltpu.VMEM((2, 4, 4, block, HD), BF),
            pltpu.VMEM((4, block, HD), BF),
            pltpu.VMEM((4, orows, ow), BF),
            pltpu.VMEM((2 * block, 4 * orows), BF),
            pltpu.VMEM((4, block, ow), BF),
            pltpu.VMEM((2, 2, block // 4, ow), BF),
            pltpu.VMEM((2, block, ow), BF),
            pltpu.VMEM((block, ow), F32),
            pltpu.SemaphoreType.DMA((N_SENDS,)),
            pltpu.SemaphoreType.DMA((N_MESSAGES,)),
            pltpu.SemaphoreType.DMA((N_LOCAL,)),
        ],
        compiler_params=pltpu.CompilerParams(
            collective_id=0, has_side_effects=True, vmem_limit_bytes=62 * 1024 * 1024
        ),
    )(hidden, w_query, w_key, w_value, w_out, norm_gain.reshape(width // HD, HD), tables)


def solution(mesh):
    cube = Mesh(mesh.devices.reshape(4, 4, 4, 2), ("z", "y", "x", "c"))
    rows, cols = ("z", "y"), ("x", "c")
    both = P(rows, cols)
    return jax.shard_map(
        on_device,
        mesh=cube,
        in_specs=(both, P(cols), both, both, both, both),
        out_specs=(both, both),
        check_vma=False,
    )
```

```python
import math

import jax
import jax.numpy as jnp
import numpy as np
from jax import lax
from jax.experimental import pallas as pl
from jax.experimental.pallas import tpu as pltpu
from jax.sharding import Mesh, PartitionSpec as P

HD = 128
EPS = 1e-5
MESH = pl.DeviceIdType.MESH
BF = jnp.bfloat16
F32 = jnp.float32


def rotary_tables(block, blocks):
    freqs = np.exp(-math.log(10000.0) * 2.0 * np.arange(HD // 2) / HD)
    freqs = np.concatenate([freqs, freqs])[None, :]
    base = (np.arange(blocks) * block)[:, None] * freqs
    rows = np.arange(block)[:, None] * freqs
    angles = np.concatenate([base, rows], axis=0)
    return np.concatenate([np.cos(angles), np.sin(angles)], axis=1).astype(np.float32)


class Ids:
    def __init__(self):
        self.table = {}

    def __call__(self, *name):
        return self.table.setdefault(name, len(self.table))


N_MESSAGES = 91
N_LOCAL = 9
N_SENDS = 20


def kernel(
    features, hidden, wq, wk, wv, wout, gain, table_in,
    ctx_out, layer_out,
    big, transit, gbuf, tables, xs, ssq, sqs, rsc, wg, pbuf, tr, fin, kvg, qbuf, sbuf,
    probs, cown, cx, ctxs, wog, lhs, op, otr, ofin, oacc, send_sem, recv_sem, local_sem,
):
    z, y, x, c = (lax.axis_index(n) for n in ("z", "y", "x", "c"))
    zr, zl, zf = (lax.rem(z + k, 4) for k in (1, 3, 2))
    yr, yl, yf = (lax.rem(y + k, 4) for k in (1, 3, 2))
    xr, xl, xf = (lax.rem(x + k, 4) for k in (1, 3, 2))
    other = 1 - c
    block = hidden.shape[0]
    half = block // 2
    ids, local_ids, small = Ids(), Ids(), Ids()
    unit = big.shape[1] * big.shape[2] // 8
    groups, classes = (2, 4, 8, 9), {}
    gathered = ("wk", "wv", "wq", "k", "v", "wo")
    order = {"k": 0, "v": 1, "q": 2}
    sends = []

    def group_of(src):
        size = math.prod(src.shape) * src.dtype.itemsize
        return size // unit if size % unit == 0 else 0

    def arrival(name):
        if name[0] in gathered and name[1:] in (("r", 1), ("l", 0), ("fr",), ("fl",)):
            return name[0], "rest"
        if name[0] in order and name[1] in ("a0", "a1", "b0", "b1"):
            return name[0], "sum"
        if name[0] == "cp":
            return "cp", name[2]
        return name

    def message(src, dst, name, **where):
        i = ids(*arrival(name))
        g = group_of(src)
        g = 9 if g == 8 and name[0][0] == "w" else g
        g = 0 if name[0] == "swap" else g
        classes[i] = g
        shared = groups.index(g) if g in groups else len(groups) + small(*name)
        return pltpu.make_async_remote_copy(
            src_ref=src, dst_ref=dst, send_sem=send_sem.at[shared], recv_sem=recv_sem.at[i],
            device_id=where, device_id_type=MESH,
        )

    def send(src, dst, name, **where):
        copy = message(src, dst, name, **where)
        copy.start()
        sends.append((name, copy))

    def drain():
        counts = {}
        for name, copy in sends:
            g = classes[ids(*arrival(name))]
            if g in groups:
                counts[g] = counts.get(g, 0) + 1
            else:
                copy.wait_send()
        for g, count in counts.items():
            lines_out = count * min(g, 8) * unit // (2 * big.shape[2])
            slots = max(n for n in range(1, 13) if lines_out % (16 * n) == 0 and lines_out // n <= big.shape[1])
            ref = big.at[pl.ds(0, slots), pl.ds(0, lines_out // slots)]
            pltpu.make_async_remote_copy(
                src_ref=ref, dst_ref=ref, send_sem=send_sem.at[groups.index(g)],
                recv_sem=recv_sem.at[0], device_id={"c": other}, device_id_type=MESH,
            ).wait_send()

    def arrived(dst, name, **where):
        pltpu.make_async_remote_copy(
            src_ref=dst, dst_ref=dst, send_sem=send_sem.at[0], recv_sem=recv_sem.at[ids(*arrival(name))],
            device_id=where, device_id_type=MESH,
        ).wait_recv()

    barrier = pltpu.get_barrier_semaphore()
    partners = [{"z": zr}, {"z": zl}, {"z": zf}, {"y": yr}, {"y": yl}, {"x": xr}, {"x": xl}, {"c": other}]
    for where in partners:
        pl.semaphore_signal(barrier, inc=1, device_id=where, device_id_type=MESH)

    def load(src, dst, name):
        copy = pltpu.make_async_copy(src, dst, local_sem.at[local_ids("load", name)])
        copy.start()
        return copy

    weights = {"k": wk, "v": wv, "q": wq}
    order = {"k": 0, "v": 1, "q": 2}
    score_factor = math.log2(math.e) / math.sqrt(HD)
    loads = {"x": load(hidden, big.at[x], "x")}
    for name in "kvq":
        loads[name] = load(weights[name], wg.at[order[name], y], name)
    loads["o"] = load(wout, wog.at[y], "o")
    loads["g"] = load(gain, gbuf.at[x, c], "g")
    loads["t"] = load(table_in, tables, "t")
    pl.semaphore_wait(barrier, len(partners))

    lines = {"y": (y, yr, yl, yf), "z": (z, zr, zl, zf)}

    def gather(axis, slot, name, pieces=(0, 1)):
        me, right, left, _ = lines[axis]
        for n in pieces:
            for h, side, to in ((n, "r", right), (1 - n, "l", left)):
                send(slot(me, h), slot(me, h), (name, side, h), **{axis: to})

    def forward(axis, slot, name):
        _, right, left, _ = lines[axis]
        arrived(slot(left, 0), (name, "r", 0), **{axis: right})
        send(slot(left, 0), slot(left, 0), (name, "fr"), **{axis: right})
        arrived(slot(right, 1), (name, "l", 1), **{axis: left})
        send(slot(right, 1), slot(right, 1), (name, "fl"), **{axis: left})

    def finish(axis, slot, name):
        if name in ("k", "v"):
            rest = kvg.at[0 if name == "k" else 1, :, pl.ds(0, 2)]
        else:
            rest = wog.at[pl.ds(0, 2)] if name == "wo" else wg.at[order[name[1]], pl.ds(0, 2)]
        arrived(rest, (name, "rest"), c=other)

    def gather_y(slot, name):
        gather("y", slot, name)

    def forward_y(slot, name):
        forward("y", slot, name)

    def finish_y(slot, name):
        finish("y", slot, name)

    wrows = wk.shape[0]

    def weight_slot(name):
        def slot(owner, part):
            ref = wg.at[order[name], owner]
            return ref if part is None else ref.at[pl.ds(part * (wrows // 2), wrows // 2)]
        return slot

    class Spread:
        def __init__(self, name, buf, through):
            self.name, self.buf, self.through = name, buf, through
            self.rows = buf.shape[1] // 2

        def part(self, slot, h):
            return self.buf.at[slot, pl.ds(h * self.rows, self.rows)]

        def own(self):
            for h, side, to in ((0, "xr", xr), (1, "xl", xl), (1, "xr", xr), (0, "xl", xl)):
                mine = self.part(x, h)
                send(mine, mine, (self.name, side, h), x=to)
            self.onward(0, 0)
            self.onward(0, 1)

        def pair(self, src_slot, owner, label, h):
            send(self.part(src_slot, h), self.part(8 + owner, h), (self.name, "pair", label, h), c=other)

        def onward(self, k, h):
            owner = lax.rem(x + k, 4)
            away = lax.rem(owner - z + 4, 4)
            src = self.part(owner, h)

            @pl.when(away == 0)
            def _():
                message(src, self.part(8 + z, h), (self.name, "pair", "own", h), c=other).start()

            @pl.when(away == 1)
            def _():
                message(src, self.part(4 + z, h), (self.name, "zr", h), z=zr).start()

            @pl.when(away == 3)
            def _():
                message(src, self.part(4 + z, h), (self.name, "zl", h), z=zl).start()

            @pl.when(away == 2)
            def _():
                to = {"z": zl} if h else {"z": zr}
                message(src, self.through.at[h], (self.name, "zz", h), **to).start()

            if k == 0:
                for label, where in (("zr", {"z": zr}), ("zl", {"z": zl}), ("zz", {"z": zl} if h else {"z": zr})):
                    name = (self.name, label, h)
                    sends.append((name, message(self.part(0, h), self.part(0, h), name, **where)))
                name = (self.name, "pair", "own", h)
                sends.append((name, message(self.part(0, h), self.part(0, h), name, c=other)))

        def from_left(self, h):
            mine = self.part(xl, h)
            arrived(mine, (self.name, "xr", h), x=xr)
            if h == 0:
                send(mine, mine, (self.name, "xf", 0), x=xr)
            self.onward(3, h)

        def from_right(self, h):
            mine = self.part(xr, h)
            arrived(mine, (self.name, "xl", h), x=xl)
            if h == 1:
                send(mine, mine, (self.name, "xf", 1), x=xl)
            self.onward(1, h)

        def from_far(self, h):
            where = {"x": xl} if h else {"x": xr}
            arrived(self.part(xf, h), (self.name, "xf", h), **where)
            self.onward(2, h)

        def pass_on(self, h):
            where = {"z": zl} if h else {"z": zr}
            arrived(self.through.at[h], (self.name, "zz", h), **where)
            send(self.through.at[h], self.part(4 + (zr if h else zl), h), (self.name, "zf", h), **where)

        def beside(self, which, h):
            owner, where = (zl, {"z": zr}) if which == "zr" else (zr, {"z": zl})
            arrived(self.part(4 + owner, h), (self.name, which, h), **where)
            self.pair(4 + owner, owner, which, h)

        def opposite(self, h):
            where = {"z": zl} if h else {"z": zr}
            arrived(self.part(4 + zf, h), (self.name, "zf", h), **where)
            self.pair(4 + zf, zf, "zf", h)

        def paired(self, owner, label):
            for h in range(2):
                arrived(self.part(8 + owner, h), (self.name, "pair", label, h), c=other)

    def process(slot, plane, t, first):
        g = gbuf[z, plane].astype(F32)
        width = big.shape[2]

        @pl.loop(0, block // 32)
        def _(i):
            r = pl.ds(pl.multiple_of(i * 32, 32), 32)
            total = None
            for k in range(width // HD):
                cols = slice(k * HD, (k + 1) * HD)
                v = big[slot, r, cols].astype(F32)
                xs[plane, t, r, cols] = (v * g[k:k + 1, :]).astype(BF)
                total = v * v if total is None else total + v * v
            if first:
                ssq[t, r, :] = total
            else:
                ssq[t, r, :] = ssq[t, r, :] + total

    spread = Spread("h", big, transit)
    loads["x"].wait()
    spread.own()
    loads["k"].wait()
    gather_y(weight_slot("k"), "wk")
    loads["v"].wait()
    gather_y(weight_slot("v"), "wv")
    loads["g"].wait()
    gain_sends = [("r", {"x": xr}), ("l", {"x": xl}), ("c", {"c": other})]
    for label, where in gain_sends:
        send(gbuf.at[x, c], gbuf.at[x, c], ("gain", label), **where)
    spread.from_left(0)
    spread.from_right(1)
    spread.from_right(0)
    spread.from_left(1)
    arrived(gbuf.at[xl, c], ("gain", "r"), x=xr)
    send(gbuf.at[xl, c], gbuf.at[xl, c], ("gain", "rf"), x=xr)
    send(gbuf.at[xl, c], gbuf.at[xl, c], ("gain", "rc"), c=other)
    arrived(gbuf.at[xr, c], ("gain", "l"), x=xl)
    send(gbuf.at[xr, c], gbuf.at[xr, c], ("gain", "lc"), c=other)
    forward_y(weight_slot("k"), "wk")
    spread.from_far(0)
    spread.from_far(1)
    arrived(gbuf.at[xf, c], ("gain", "rf"), x=xr)
    send(gbuf.at[xf, c], gbuf.at[xf, c], ("gain", "fc"), c=other)
    spread.pass_on(0)
    spread.pass_on(1)
    arrived(gbuf.at[x, other], ("gain", "c"), c=other)
    arrived(gbuf.at[xl, other], ("gain", "rc"), c=other)
    arrived(gbuf.at[xr, other], ("gain", "lc"), c=other)
    arrived(gbuf.at[xf, other], ("gain", "fc"), c=other)
    process(z, c, z, True)
    forward_y(weight_slot("v"), "wv")
    loads["q"].wait()
    gather_y(weight_slot("q"), "wq")
    for which, owner in (("zr", zl), ("zl", zr)):
        for h in range(2):
            spread.beside(which, h)
        process(4 + owner, c, owner, True)
    spread.paired(z, "own")
    process(8 + z, other, z, False)
    for h in range(2):
        spread.opposite(h)
    process(4 + zf, c, zf, True)
    for label, owner in (("zr", zl), ("zl", zr), ("zf", zf)):
        spread.paired(owner, label)
        process(8 + owner, other, owner, False)
    for t in range(4):
        s = jnp.sum(ssq[t].T, axis=0, keepdims=True)
        sqs[z, t] = jnp.broadcast_to(s, (8, block))
    for where, label in ((zr, 1), (zl, 3), (zf, 2)):
        send(sqs.at[z], sqs.at[z], ("sq", label), z=where)

    cw = wk.shape[1]

    def lower(ref):
        return ref.at[pl.ds(0, 2 * block)]

    def upper(ref):
        return ref.at[pl.ds(2 * block, 2 * block)]

    def project(name):
        j = order[name]
        width = xs.shape[3]
        tokens = 4 * block

        @pl.loop(0, cw // 256)
        def _(n):
            cols = pl.ds(pl.multiple_of(n * 256, 256), 256)
            w0 = wg[j, 0:2, :, cols].reshape(width, 256)
            w1 = wg[j, 2:4, :, cols].reshape(width, 256)
            left0 = xs[0].reshape(tokens, width)
            left1 = xs[1].reshape(tokens, width)
            acc = jnp.dot(left0, w0, preferred_element_type=F32)
            acc = acc + jnp.dot(left1, w1, preferred_element_type=F32)
            pbuf[j, 2 * n] = acc[:, :HD].astype(BF)
            pbuf[j, 2 * n + 1] = acc[:, HD:].astype(BF)

    def scatter(name):
        j = order[name]
        send(lower(pbuf.at[j, zf]), tr.at[j, 0], (name, "ta"), z=zr)
        send(upper(pbuf.at[j, zf]), tr.at[j, 1], (name, "tb"), z=zl)
        send(upper(pbuf.at[j, zr]), upper(fin.at[j, 0]), (name, "a1"), z=zr)
        send(lower(pbuf.at[j, zl]), lower(fin.at[j, 1]), (name, "b0"), z=zl)

    def relay(name):
        j = order[name]
        lo, hi = pl.ds(0, 2 * block), pl.ds(2 * block, 2 * block)
        arrived(tr.at[j, 0], (name, "ta"), z=zr)
        pbuf[j, zr, lo, :] = (pbuf[j, zr, lo, :].astype(F32) + tr[j, 0].astype(F32)).astype(BF)
        send(lower(pbuf.at[j, zr]), lower(fin.at[j, 0]), (name, "a0"), z=zr)
        arrived(tr.at[j, 1], (name, "tb"), z=zl)
        pbuf[j, zl, hi, :] = (pbuf[j, zl, hi, :].astype(F32) + tr[j, 1].astype(F32)).astype(BF)
        send(upper(pbuf.at[j, zl]), upper(fin.at[j, 1]), (name, "b1"), z=zl)

    def reduced(name):
        j = order[name]
        arrived(fin.at[j], (name, "sum"), c=other)

    def total_of(name, t):
        j = order[name]
        r = pl.ds(t * block, block)
        total = pbuf[j, z, r, :].astype(F32) + fin[j, 0, r, :].astype(F32) + fin[j, 1, r, :].astype(F32)
        return total * rsc[r, :]

    def rotated(v, t):
        bases = tables[:16, :]
        here = lax.broadcasted_iota(jnp.int32, bases.shape, 0) == 4 * t + y
        base = jnp.sum(jnp.where(here, bases, 0.0), axis=0, keepdims=True)
        ca, sa = base[:, :HD], base[:, HD:]
        ci, si = tables[16:, :HD], tables[16:, HD:]
        cos = ca * ci - sa * si
        sin = sa * ci + ca * si
        lane = lax.broadcasted_iota(jnp.int32, (block, HD), 1)
        signed = jnp.where(lane < HD // 2, -sin, sin)
        return v * cos + pltpu.roll(v, HD // 2, axis=1) * signed

    finish_y(weight_slot("k"), "wk")
    project("k")
    scatter("k")
    finish_y(weight_slot("v"), "wv")
    project("v")
    relay("k")
    scatter("v")

    for where, label in ((zr, 1), (zl, 3), (zf, 2)):
        src = {1: zl, 3: zr, 2: zf}[label]
        arrived(sqs.at[src], ("sq", label), z=where)
    for t in range(4):
        s = sqs[0, t] + sqs[1, t] + sqs[2, t] + sqs[3, t]
        factor = lax.rsqrt(s / features + EPS)
        rsc[pl.ds(t * block, block), :] = jnp.broadcast_to(factor[0:1, :], (HD, block)).T

    def kv_slot(which):
        def slot(owner, part):
            ref = kvg.at[which]
            return ref.at[:, owner] if part is None else ref.at[pl.ds(2 * part, 2), owner]
        return slot

    def out_slot(owner, part):
        ref = wog.at[owner]
        count = wout.shape[0] // 2
        return ref if part is None else ref.at[pl.ds(part * count, count)]

    forward_y(weight_slot("q"), "wq")
    loads["t"].wait()
    reduced("k")
    for t in range(4):
        kvg[0, t, y] = rotated(total_of("k", t), t).astype(BF)
    gather_y(kv_slot(0), "k")
    relay("v")
    finish_y(weight_slot("q"), "wq")
    project("q")
    scatter("q")
    forward_y(kv_slot(0), "k")
    reduced("v")
    for t in range(4):
        kvg[1, t, y] = total_of("v", t).astype(BF)
    gather_y(kv_slot(1), "v")
    relay("q")
    loads["o"].wait()
    forward_y(kv_slot(1), "v")
    gather("y", out_slot, "wo")
    reduced("q")
    for t in range(4):
        qbuf[t] = (rotated(total_of("q", t), t) * score_factor).astype(BF)
    finish_y(kv_slot(0), "k")

    span = 4 * block

    def keys(which, kb):
        return kvg[which, kb].reshape(span, HD)

    def base_of(name):
        return [ids(*name, k) for k in range(4)][0]

    def direct(src, dst, name, to, source, **where):
        first = base_of(name)
        small_base = [small(*name, k) for k in range(4)][0]
        return pltpu.make_async_remote_copy(
            src_ref=src, dst_ref=dst, send_sem=send_sem.at[len(groups) + small_base + to],
            recv_sem=recv_sem.at[first + source], device_id=where, device_id_type=MESH,
        )

    def rows_of(part):
        return pl.ds(part * half, half)

    def score_rows(part):
        mine = rows_of(part)
        for t in range(4):
            q = qbuf[t, mine, :]
            peak = None
            for kb in range(t + 1):
                s = lax.dot_general(q, keys(0, kb), (((1,), (1,)), ((), ())), preferred_element_type=F32)
                if kb == t:
                    row = lax.broadcasted_iota(jnp.int32, (half, span), 0) + (y * block + part * half)
                    col = lax.broadcasted_iota(jnp.int32, (half, span), 1)
                    s = jnp.where(col <= row, s, -jnp.inf)
                sbuf[t, kb] = s
                here = jnp.max(s, axis=1, keepdims=True)
                peak = here if peak is None else jnp.maximum(peak, here)
            for kb in range(t + 1):
                cols = slice(kb * span, (kb + 1) * span)
                probs[t, :, cols] = jnp.exp2(sbuf[t, kb] - peak).astype(BF)

    def context_rows(part):
        mine = rows_of(part)
        ones = jnp.ones((span, HD), BF)
        for t in range(4):
            acc = jnp.zeros((half, 2 * HD), F32)
            for kb in range(t + 1):
                right = jnp.concatenate([keys(1, kb), ones], axis=1)
                cols = slice(kb * span, (kb + 1) * span)
                acc = acc + jnp.dot(probs[t, :, cols], right, preferred_element_type=F32)
            cown[t, mine, :] = (acc[:, :HD] / acc[:, HD:]).astype(BF)
        swap(part, True)

    def swap(part, start):
        mine = rows_of(part)
        src, dst = cown.at[:, mine], cx.at[c, z, :, mine]
        copy = message(src, dst, ("swap", part), z=x, x=z)
        local = pltpu.make_async_copy(src, cx.at[c, x, :, mine], local_sem.at[local_ids("swap", part)])

        @pl.when(x != z)
        def _():
            if start:
                copy.start()
            else:
                copy.wait_recv()
                copy.wait_send()

        @pl.when(x == z)
        def _():
            if start:
                local.start()
            else:
                local.wait()

    def cx_part(plane, owner, part, h):
        return cx.at[plane, owner, pl.ds(2 * h, 2), rows_of(part)]

    def cx_pair(owner, label, part, h):
        mine = cx_part(c, owner, part, h)
        send(mine, mine, ("cp", label, part, h), c=other)

    def context_around(part):
        swap(part, False)
        for h, side, where in ((0, "cr", {"x": xr}), (1, "cl", {"x": xl}), (1, "cr", {"x": xr}), (0, "cl", {"x": xl})):
            send(cx_part(c, x, part, h), cx_part(c, x, part, h), (side, part, h), **where)
        for h in range(2):
            cx_pair(x, "own", part, h)

    def context_beside(part):
        left, right = cx_part(c, xl, part, 0), cx_part(c, xr, part, 1)
        arrived(left, ("cr", part, 0), x=xr)
        send(left, left, ("cf", part, 0), x=xr)
        cx_pair(xl, "left", part, 0)
        arrived(right, ("cl", part, 1), x=xl)
        send(right, right, ("cf", part, 1), x=xl)
        cx_pair(xr, "right", part, 1)

    def context_far(part):
        arrived(cx_part(c, xl, part, 1), ("cr", part, 1), x=xr)
        cx_pair(xl, "left", part, 1)
        arrived(cx_part(c, xr, part, 0), ("cl", part, 0), x=xl)
        cx_pair(xr, "right", part, 0)
        arrived(cx_part(c, xf, part, 0), ("cf", part, 0), x=xr)
        cx_pair(xf, "far", part, 0)
        arrived(cx_part(c, xf, part, 1), ("cf", part, 1), x=xl)
        cx_pair(xf, "far", part, 1)

    targets = (zf, zr, zl, z)

    def out_product(part):
        mine = rows_of(part)
        arrived(cx.at[other, :, :, mine], ("cp", "any", part), c=other)
        depth = lhs.shape[1]

        def product(first_target, count):
            for i in range(first_target, first_target + count):
                for k in range(4):
                    for p in range(2):
                        lhs[i * half:(i + 1) * half, (4 * p + k) * HD:(4 * p + k + 1) * HD] = cx[p, k, targets[i], mine, :]

            @pl.loop(0, wog.shape[2] // 256)
            def _(n):
                cols = pl.ds(pl.multiple_of(n * 256, 256), 256)
                left = lhs[first_target * half:(first_target + count) * half, :]
                acc = jnp.dot(left, wog[:, :, cols].reshape(depth, 256), preferred_element_type=F32)
                for i in range(first_target, first_target + count):
                    rows = slice((i - first_target) * half, (i - first_target + 1) * half)
                    if i < 3:
                        op[targets[i], mine, cols] = acc[rows].astype(BF)
                    else:
                        oacc[mine, cols] = acc[rows]

        if part == 0:
            product(0, 1)
            out_across(part)
            product(1, 3)
            out_scatter(part)
        else:
            product(0, 4)

    quarter = half // 2

    def piece(part, h):
        return pl.ds(part * half + h * quarter, quarter)

    def out_across(part):
        send(op.at[zf, piece(part, 0)], otr.at[part, 0], ("o", part, "ta"), z=zr)
        send(op.at[zf, piece(part, 1)], otr.at[part, 1], ("o", part, "tb"), z=zl)

    def out_scatter(part):
        send(op.at[zr, piece(part, 1)], ofin.at[0, piece(part, 1)], ("o", part, "a1"), z=zr)
        send(op.at[zl, piece(part, 0)], ofin.at[1, piece(part, 0)], ("o", part, "b0"), z=zl)

    def out_relay(part):
        for h, to, where, came, name in ((0, zr, {"z": zr}, "ta", "a0"), (1, zl, {"z": zl}, "tb", "b1")):
            r = piece(part, h)
            arrived(otr.at[part, h], ("o", part, came), **where)
            op[to, r, :] = (op[to, r, :].astype(F32) + otr[part, h].astype(F32)).astype(BF)
            send(op.at[to, r], ofin.at[h, r], ("o", part, name), **where)

    def out_finish(part):
        arrived(ofin.at[0, piece(part, 1)], ("o", part, "a1"), z=zr)
        arrived(ofin.at[1, piece(part, 0)], ("o", part, "b0"), z=zl)
        for h, name, where in ((0, "a0", {"z": zr}), (1, "b1", {"z": zl})):
            r = piece(part, h)
            arrived(ofin.at[h, r], ("o", part, name), **where)
            total = big[x, r, :].astype(F32) + oacc[r, :]
            layer_out[r, :] = (total + ofin[0, r, :].astype(F32) + ofin[1, r, :].astype(F32)).astype(BF)

    score_rows(0)
    finish_y(kv_slot(1), "v")
    context_rows(0)
    score_rows(1)
    forward("y", out_slot, "wo")
    context_rows(1)
    context_around(0)
    for t in range(4):
        @pl.when(z != t)
        def _():
            direct(cown.at[t], ctxs.at[z], ("c2",), t, z, z=t).start()

        @pl.when(z == t)
        def _():
            ctxs[z] = cown[t]

    context_beside(0)
    context_around(1)
    context_far(0)
    finish("y", out_slot, "wo")
    out_product(0)
    context_beside(1)
    context_far(1)
    out_relay(0)
    out_product(1)
    out_across(1)
    out_scatter(1)

    for h in range(4):
        @pl.when(z != h)
        def _():
            copy = direct(ctxs.at[h], ctxs.at[h], ("c2",), h, h, z=h)
            copy.wait_send()
            copy.wait_recv()

        ctx_out[:, h * HD:(h + 1) * HD] = ctxs[h]

    out_finish(0)
    out_relay(1)
    out_finish(1)
    drain()


def on_device(hidden, norm_gain, w_query, w_key, w_value, w_out):
    block, width = hidden.shape
    wrows, cw = w_query.shape
    orows, ow = w_out.shape
    features = 8 * width
    tables = jnp.asarray(rotary_tables(block, 16))

    def body(*refs):
        kernel(features, *refs)

    return pl.pallas_call(
        body,
        out_shape=(
            pltpu.VMEM((block, cw), BF),
            pltpu.VMEM((block, ow), BF),
        ),
        in_specs=[pl.BlockSpec(memory_space=pl.ANY)] * 7,
        out_specs=(pl.BlockSpec(memory_space=pltpu.VMEM),) * 2,
        scratch_shapes=[
            pltpu.VMEM((12, block, width), BF),
            pltpu.VMEM((2, block // 2, width), BF),
            pltpu.VMEM((4, 2, width // HD, HD), BF),
            pltpu.VMEM((16 + block, 2 * HD), F32),
            pltpu.VMEM((2, 4, block, width), BF),
            pltpu.VMEM((4, block, HD), F32),
            pltpu.VMEM((4, 4, 8, block), F32),
            pltpu.VMEM((4 * block, HD), F32),
            pltpu.VMEM((3, 4, wrows, cw), BF),
            pltpu.VMEM((3, 4, 4 * block, HD), BF),
            pltpu.VMEM((3, 2, 2 * block, HD), BF),
            pltpu.VMEM((3, 2, 4 * block, HD), BF),
            pltpu.VMEM((2, 4, 4, block, HD), BF),
            pltpu.VMEM((4, block, HD), BF),
            pltpu.VMEM((4, 4, block // 2, 4 * block), F32),
            pltpu.VMEM((4, block // 2, 16 * block), BF),
            pltpu.VMEM((4, block, HD), BF),
            pltpu.VMEM((2, 4, 4, block, HD), BF),
            pltpu.VMEM((4, block, HD), BF),
            pltpu.VMEM((4, orows, ow), BF),
            pltpu.VMEM((2 * block, 4 * orows), BF),
            pltpu.VMEM((4, block, ow), BF),
            pltpu.VMEM((2, 2, block // 4, ow), BF),
            pltpu.VMEM((2, block, ow), BF),
            pltpu.VMEM((block, ow), F32),
            pltpu.SemaphoreType.DMA((N_SENDS,)),
            pltpu.SemaphoreType.DMA((N_MESSAGES,)),
            pltpu.SemaphoreType.DMA((N_LOCAL,)),
        ],
        compiler_params=pltpu.CompilerParams(
            collective_id=0, has_side_effects=True, vmem_limit_bytes=62 * 1024 * 1024
        ),
    )(hidden, w_query, w_key, w_value, w_out, norm_gain.reshape(width // HD, HD), tables)


def solution(mesh):
    cube = Mesh(mesh.devices.reshape(4, 4, 4, 2), ("z", "y", "x", "c"))
    rows, cols = ("z", "y"), ("x", "c")
    both = P(rows, cols)
    return jax.shard_map(
        on_device,
        mesh=cube,
        in_specs=(both, P(cols), both, both, both, both),
        out_specs=(both, both),
        check_vma=False,
    )
```
